128 devices in a mesh: bulk: 8 (over y, core), front: 16 (over x, z).
Axes of the slice: x: 4, y: 4, z: 4, core: 2. Of those that a mesh axis runs over, the one named last changes fastest.
Arguments:
- child_pivot: float32 [8, 2048, 2048], P('bulk', 'front'), may hold values from -20 to 40, as said below
- child_coupling: float32 [8, 2048, 2048], P('bulk', 'front'), may hold values from -0.75 to 0.75
- parent_arrow: float32 [8192, 1024], P(('bulk', 'front')), may hold values from -600 to 3000, as said below
- row_map: int32 [8, 2048], P('bulk', 'front'), may hold values from 0 to 8191, as said below
- block_pattern: int32 [64, 8], replicated, may hold values from 0 to 1, as said below
Outputs:
- child_factor_pivot: float32 [8, 2048, 2048], P('bulk', 'front')
- child_factor_coupling: float32 [8, 2048, 2048], P('bulk', 'front')
- parent_factor: float32 [8192, 1024], P(('bulk', 'front'))
The draws below stay inside these ranges and needn't reach their ends.
Inputs may be any that keep to these rules, and one draw needn't show every extreme that they name: `child_pivot`: each child's matrix is symmetric and positive definite. `parent_arrow`: the first 1024 rows hold a symmetric block that stays positive definite when contribution is added. `row_map`: A child's 2048 entries are distinct. Entry i of a child names a row r with (r // 64) % (16) == i // 128. `block_pattern`: every block (i, i) with i < 8 is 1.
All inputs are finite; a program needn't handle non-finite values.
Results may differ from the reference program's by a relative error of at most 0.00022.
Values sent between devices are 32-bit elements; how exact they have to be, the bound alone decides.
A program may use at most 128 MiB of HBM per device.

```python
import jax
import jax.numpy as jnp
from jax import lax

EC = 2048
UC = 2048
PO = 8192
PE = 1024
BLOCK = 128
CHILDREN = 8
N_BULK = 8
N_FRONT = 16


def draw_child_pivot(key, part):
    key_basis, key_shift = jax.random.split(key, 2)
    samples = EC + EC // 4
    basis = jax.random.normal(key_basis, (N_BULK, EC, samples), jnp.float32)
    gram = jnp.einsum('cik,cjk->cij', basis, basis, precision=lax.Precision.HIGHEST) / samples
    shift = jax.random.uniform(key_shift, (N_BULK, EC), jnp.float32, 0.02, 0.08)
    matrix = gram + shift[:, :, None] * jnp.eye(EC, dtype=jnp.float32)[None]
    return matrix


def draw_parent_arrow(key, part):
    key_top, key_diag, key_rest = jax.random.split(key, 3)
    samples = PE + PE // 4
    basis = jax.random.normal(key_top, (PE, samples), jnp.float32)
    gram = jnp.dot(basis, basis.T, precision=lax.Precision.HIGHEST) / samples
    offset = jax.random.uniform(key_diag, (PE,), jnp.float32, 150.0, 250.0)
    upper_block = 500.0 * gram + jnp.diag(offset)
    lower_rows = jnp.clip(3.0 * jax.random.normal(key_rest, (PO - PE, PE), jnp.float32), -18.0, 18.0)
    return jnp.concatenate([upper_block, lower_rows], axis=0)


def draw_row_map(key, part):
    row_count = PO // (N_BULK * N_FRONT)
    candidates = N_BULK * row_count
    per_block = UC // N_FRONT
    forced = jnp.full((N_BULK * N_FRONT,), -1, jnp.int32).at[0].set(0).at[N_FRONT - 1].set(candidates - 1)
    block_keys = jax.random.split(key, N_BULK * N_FRONT)

    def pick_rows(one_key, forced_value):
        order = jax.random.permutation(one_key, candidates).astype(jnp.int32)
        where_forced = jnp.argmax(order == forced_value)
        leading = order[0]
        order = order.at[where_forced].set(leading)
        order = order.at[0].set(jnp.where(forced_value >= 0, forced_value, leading))
        return order[:per_block]
    chosen = jax.vmap(pick_rows)(block_keys, forced).reshape(N_BULK, N_FRONT, per_block)
    group_index = chosen // row_count
    inside = chosen % row_count
    front_index = jnp.arange(N_FRONT, dtype=jnp.int32)[None, :, None]
    parent_rows = (group_index * N_FRONT + front_index) * row_count + inside
    return parent_rows.reshape(N_BULK, UC).astype(jnp.int32)


def draw_block_pattern(key, part):
    block_rows = PO // BLOCK
    block_cols = PE // BLOCK
    levels = jax.random.randint(key, (block_rows, block_cols), 0, 4)
    present = levels > 0
    on_diagonal = jnp.arange(block_rows)[:, None] == jnp.arange(block_cols)[None, :]
    return jnp.where(on_diagonal | present, 1, 0).astype(jnp.int32)


def shard_levels(rng, extent, cuts, least, high):
    gain = 1.0
    for axis_at, shards_of in cuts:
        heights = jax.random.uniform(jax.random.fold_in(jax.random.fold_in(rng, 6), axis_at), (shards_of,), jnp.float32, least / len(cuts), high / len(cuts))
        gain = gain * jnp.repeat(jnp.exp(heights), extent[axis_at] // shards_of).reshape((-1,) + (1,) * (len(extent) - 1 - axis_at))
    return gain


def noise(rng, extent, scale, limit, cuts=(), held_as=jnp.bfloat16):
    values = jax.random.normal(rng, extent, jnp.float32) * scale
    if len(cuts) > 0:
        values = shard_levels(rng, extent, cuts, -0.22, 0.18) * values
    return jnp.clip(values, min=-limit, max=limit).astype(held_as)


def setup_inputs(seed: int = 0) -> dict:
    arg_keys = jax.random.split(jax.random.key(seed), 6)
    return {
        "child_pivot": draw_child_pivot(jax.random.fold_in(arg_keys[5], 71), 0),
        "child_coupling": noise(arg_keys[1], (CHILDREN, UC, EC), (2.3 * EC ** -0.5), 0.75, ((0, 8), (1, 16)), jnp.float32),
        "parent_arrow": draw_parent_arrow(jax.random.fold_in(arg_keys[5], 71), 0),
        "row_map": draw_row_map(jax.random.fold_in(arg_keys[5], 71), 0),
        "block_pattern": draw_block_pattern(jax.random.fold_in(arg_keys[5], 71), 0),
    }


HIGHEST_PRECISION = lax.Precision.HIGHEST

def mirror_lower(matrix):
    return jnp.tril(matrix) + jnp.tril(matrix, -1).T

def reference(child_pivot, child_coupling, parent_arrow, row_map, block_pattern):

    def factor_child(operands):
        pivot_block, coupling_rows = operands
        lower_factor = jnp.linalg.cholesky(mirror_lower(pivot_block))
        coupling = jax.scipy.linalg.solve_triangular(lower_factor, coupling_rows.T, lower=True).T
        return (lower_factor, coupling)
    factors, couplings = lax.map(factor_child, (child_pivot, child_coupling))

    def add_child(total, operands):
        coupling, row_index = operands
        landing_top = jnp.zeros((PE, EC), jnp.float32).at[row_index].set(coupling, mode='drop')
        term_rows = -jnp.dot(coupling, landing_top.T, precision=HIGHEST_PRECISION)
        return (total.at[row_index].add(term_rows), None)
    contribution, _ = lax.scan(add_child, jnp.zeros((PO, PE), jnp.float32), (couplings, row_map))
    full_mask = jnp.repeat(jnp.repeat(block_pattern.astype(jnp.float32), BLOCK, axis=0), BLOCK, axis=1)
    assembled = parent_arrow * full_mask + contribution
    parent_lower = jnp.linalg.cholesky(mirror_lower(assembled[:PE]))
    parent_rest = jax.scipy.linalg.solve_triangular(parent_lower, assembled[PE:].T, lower=True).T
    return (factors, couplings, jnp.concatenate([parent_lower, parent_rest], axis=0))
```

```python
import functools

import jax
import jax.numpy as jnp
from jax import lax
from jax.experimental import pallas as pl
from jax.experimental.pallas import tpu as pltpu
from jax.sharding import PartitionSpec as P

BLOCK = 128
F32, BF = jnp.float32, jnp.bfloat16
NT = (((1,), (1,)), ((), ()))
HIGHEST_PRECISION = lax.Precision.HIGHEST


def factor_block(load_row, store_u, store_e, n=128, sb=8):
    nb = n // sb
    W = [load_row(v) for v in range(nb)]
    lane = lax.broadcasted_iota(jnp.int32, (sb, n), 1)
    sub = lax.broadcasted_iota(jnp.int32, (sb, n), 0)
    for b in range(nb):
        base = b * sb
        inblk = (lane >= base) & (lane < base + sb)
        R = W[b]
        S = [jnp.broadcast_to(R[:, base + j:base + j + 1], (sb, n)) for j in range(sb)]
        F = {}
        for j in range(sb):
            for i in range(j, sb):
                F[i, j] = jnp.broadcast_to(S[j][i:i + 1, :], (sb, n))
        rinv = []
        for j in range(sb):
            r = lax.rsqrt(F[j, j])
            rinv.append(r)
            for i in range(j, sb):
                F[i, j] = F[i, j] * r
            for c in range(j + 1, sb):
                for i in range(c, sb):
                    F[i, c] = F[i, c] - F[i, j] * F[c, j]
        RI = jnp.where(inblk, (lane - base == sub).astype(jnp.float32), R)
        u = []
        for j in range(sb):
            t = jnp.broadcast_to(RI[j:j + 1, :], (sb, n))
            for m in range(j):
                t = t - F[j, m] * u[m]
            u.append(t * rinv[j])
        e = u[0]
        for j in range(1, sb):
            e = jnp.where(sub == j, u[j], e)
        store_e(b, jnp.where(lane < base + sb, e, 0.0))
        d = jnp.zeros((sb, n), jnp.float32)
        for j in range(sb):
            for c in range(j, sb):
                d = jnp.where((sub == j) & (lane == base + c), F[c, j], d)
        store_u(b, jnp.where(inblk, d, jnp.where(lane < base, 0.0, e)))
        for v in range(b + 1, nb):
            C = []
            acc = jnp.where(inblk, 0.0, W[v])
            for j in range(sb):
                c = jnp.broadcast_to(W[v][:, base + j:base + j + 1], (sb, n))
                for m in range(j):
                    c = c - C[m] * F[j, m]
                c = c * rinv[j]
                C.append(c)
                acc = acc - c * u[j]
            W[v] = acc


def split(x):
    hi = x.astype(BF)
    return hi, (x - hi.astype(F32)).astype(BF)

def dot3(ah, al, bh, bl):
    d = functools.partial(lax.dot_general, dimension_numbers=NT, preferred_element_type=F32)
    return d(ah, bh) + (d(ah, bl) + d(al, bh))

def chol_kernel(n, m, a_ref, c_ref, l_out, c_out, T, Lh, Ll, U, E, Eh, El, *, own, row0):
    full = n // 256
    row_ids = None

    def chunks(lo, body):
        def step(r, _):
            body(pl.multiple_of(r * 256, 256), 256)
            return 0
        lax.fori_loop(lo, full, step, 0)
        body(n, m)

    def stage(p, _):
        k, half = p // 2, p % 2
        for kk in range(full):
            @pl.when(p == 2 * kk)
            def _():
                def upd(r, cnt):
                    rows = pl.ds(r, cnt)
                    if isinstance(r, int) and r >= n:
                        x = c_ref[:, 256 * kk:256 * kk + 256]
                    else:
                        x = a_ref[rows, 256 * kk:256 * kk + 256]
                    if kk:
                        kr = pl.ds(256 * kk, 256)
                        x = x - dot3(Lh[rows, :256 * kk], Ll[rows, :256 * kk], Lh[kr, :256 * kk], Ll[kr, :256 * kk])
                    T[rows, :] = x
                chunks(kk, upd)
        prow = pl.multiple_of(p * 128, 128)
        pcol = pl.ds(prow, 128)
        hcol = pl.ds(pl.multiple_of(half * 128, 128), 128)

        @pl.when(half == 1)
        def _():
            qcol = pl.ds(pl.multiple_of(prow - 128, 128), 128)
            bh, bl = Lh[pcol, qcol], Ll[pcol, qcol]
            def upd(r, cnt):
                rows = pl.ds(r, cnt)
                T[rows, 128:256] = T[rows, 128:256] - dot3(Lh[rows, qcol], Ll[rows, qcol], bh, bl)
            upd(prow, 128)
            chunks(k + 1, upd)

        def su(b, x): U[pl.ds(8 * b, 8), :] = x
        def se(b, x): E[pl.ds(8 * b, 8), :] = x
        factor_block(lambda v: T[pl.ds(pl.multiple_of(prow + 8 * v, 8), 8), hcol], su, se)
        eh, el = split(E[...])
        Eh[...] = eh
        El[...] = el

        def solve(r, cnt):
            rows = pl.ds(r, cnt)
            th, tl = split(T[rows, hcol])
            x = dot3(th, tl, Eh[...], El[...])
            T[rows, hcol] = x
            xh, xl = split(x)
            Lh[rows, pcol] = xh
            Ll[rows, pcol] = xl

        @pl.when(half == 0)
        def _():
            solve(pl.multiple_of(prow + 128, 128), 128)
        chunks(k + 1, solve)
        T[pl.ds(prow, 128), hcol] = U[...].T
        c_out[:, pcol] = T[n:n + m, hcol]
        mine = T[pl.ds(pl.multiple_of(row0, own), own), hcol]
        l_out[:, pcol] = jnp.where(prow < row0 + own, mine, 0.0)
        return 0

    lax.fori_loop(0, n // 128, stage, 0)

def chol_call(n, m, own, get_row0, vmem=60 << 20):
    def kern(*refs):
        chol_kernel(n, m, *refs, own=own, row0=get_row0())
    return pl.pallas_call(
        kern,
        out_shape=[jax.ShapeDtypeStruct((own, n), F32), jax.ShapeDtypeStruct((m, n), F32)],
        in_specs=[pl.BlockSpec(memory_space=pltpu.VMEM)] * 2,
        out_specs=[pl.BlockSpec(memory_space=pltpu.VMEM)] * 2,
        scratch_shapes=[pltpu.VMEM((n + m, 256), F32), pltpu.VMEM((n + m, n), BF), pltpu.VMEM((n + m, n), BF),
                        pltpu.VMEM((128, 128), F32), pltpu.VMEM((128, 128), F32),
                        pltpu.VMEM((128, 128), BF), pltpu.VMEM((128, 128), BF)],
        compiler_params=pltpu.CompilerParams(vmem_limit_bytes=vmem),
    )


def sent_and_summed(array, axis):
    pieces = array.reshape(lax.axis_size(axis), -1, array.shape[1])
    arrived = lax.all_to_all(pieces, axis, split_axis=0, concat_axis=0, tiled=True)
    return arrived.sum(axis=0)


def on_device(child_pivot, child_coupling, parent_arrow, row_map, block_pattern):
    own_rows = child_pivot[0]
    parent_index = row_map[0]
    row_count, pivot_count = own_rows.shape
    parent_count, pivots = parent_arrow.shape
    front_index = lax.axis_index("front")
    front_groups = lax.axis_size("front")
    child_whole = lax.all_gather(own_rows, "front", axis=0, tiled=True)
    lower_rows, coupling = chol_call(
        pivot_count, row_count, row_count, lambda: lax.axis_index("front") * row_count
    )(child_whole, child_coupling[0])
    slot_index = (
        parent_index // parent_count // front_groups * parent_count + parent_index % parent_count
    )
    spread_rows = lax.axis_size("bulk") * parent_count
    routing = (slot_index[:, None] == jnp.arange(spread_rows)[None, :]).astype(F32)
    landing_piece = jnp.dot(routing[:, :parent_count].T, coupling, precision=HIGHEST_PRECISION)
    landing = lax.all_gather(landing_piece, "front", axis=0, tiled=True)
    reached = -jnp.dot(coupling, landing.T, precision=lax.Precision.HIGH)
    routed = jnp.dot(routing.T, reached, precision=HIGHEST_PRECISION)
    device_index = lax.axis_index("bulk") * front_groups + front_index
    first_row = device_index * parent_count
    block_rows = (first_row + jnp.arange(parent_count)) // BLOCK
    picker = (block_rows[:, None] == jnp.arange(block_pattern.shape[0])[None, :]).astype(F32)
    row_mask = jnp.dot(picker, block_pattern.astype(F32), precision=HIGHEST_PRECISION)
    masked = parent_arrow * jnp.repeat(row_mask, BLOCK, axis=1)
    top = routed[:parent_count] + jnp.where(lax.axis_index("bulk") == 0, masked, 0.0)
    top = lax.psum(top, "bulk")
    pivot_block = lax.all_gather(top, "front", axis=0, tiled=True)
    assembled = masked + sent_and_summed(routed, "bulk")
    factor_rows, solved = chol_call(
        pivots, parent_count, parent_count, lambda: lax.axis_index("front") * parent_count
    )(pivot_block, assembled)
    parent_rows = jnp.where(first_row < pivots, factor_rows, solved)
    return (lower_rows[None], coupling[None], parent_rows)


def solution(mesh):
    placed = (
        P("bulk", "front", None),
        P("bulk", "front", None),
        P(("bulk", "front"), None),
        P("bulk", "front"),
        P(),
    )
    return jax.shard_map(
        on_device,
        mesh=mesh,
        in_specs=placed,
        out_specs=(P("bulk", "front", None), P("bulk", "front", None), P(("bulk", "front"), None)),
        check_vma=False,
    )
```

```python
import functools

import jax
import jax.numpy as jnp
from jax import lax
from jax.experimental import pallas as pl
from jax.experimental.pallas import tpu as pltpu
from jax.sharding import PartitionSpec as P

BLOCK = 128
F32, BF = jnp.float32, jnp.bfloat16
NT = (((1,), (1,)), ((), ()))
MESH = pl.DeviceIdType.MESH
HIGHEST_PRECISION = lax.Precision.HIGHEST


def factor_block(load_row, store_u, store_e, n=128, sb=8):
    nb = n // sb
    W = [load_row(v) for v in range(nb)]
    lane = lax.broadcasted_iota(jnp.int32, (sb, n), 1)
    sub = lax.broadcasted_iota(jnp.int32, (sb, n), 0)
    for b in range(nb):
        base = b * sb
        inblk = (lane >= base) & (lane < base + sb)
        R = W[b]
        S = [jnp.broadcast_to(R[:, base + j:base + j + 1], (sb, n)) for j in range(sb)]
        F = {}
        for j in range(sb):
            for i in range(j, sb):
                F[i, j] = jnp.broadcast_to(S[j][i:i + 1, :], (sb, n))
        rinv = []
        for j in range(sb):
            r = lax.rsqrt(F[j, j])
            rinv.append(r)
            for i in range(j, sb):
                F[i, j] = F[i, j] * r
            for c in range(j + 1, sb):
                for i in range(c, sb):
                    F[i, c] = F[i, c] - F[i, j] * F[c, j]
        RI = jnp.where(inblk, (lane - base == sub).astype(jnp.float32), R)
        u = []
        for j in range(sb):
            t = jnp.broadcast_to(RI[j:j + 1, :], (sb, n))
            for m in range(j):
                t = t - F[j, m] * u[m]
            u.append(t * rinv[j])
        e = u[0]
        for j in range(1, sb):
            e = jnp.where(sub == j, u[j], e)
        store_e(b, jnp.where(lane < base + sb, e, 0.0))
        d = jnp.zeros((sb, n), jnp.float32)
        for j in range(sb):
            for c in range(j, sb):
                d = jnp.where((sub == j) & (lane == base + c), F[c, j], d)
        store_u(b, jnp.where(inblk, d, jnp.where(lane < base, 0.0, e)))
        for v in range(b + 1, nb):
            C = []
            acc = jnp.where(inblk, 0.0, W[v])
            for j in range(sb):
                c = jnp.broadcast_to(W[v][:, base + j:base + j + 1], (sb, n))
                for m in range(j):
                    c = c - C[m] * F[j, m]
                c = c * rinv[j]
                C.append(c)
                acc = acc - c * u[j]
            W[v] = acc


def split(x):
    hi = x.astype(BF)
    return hi, (x - hi.astype(F32)).astype(BF)

def dot3(ah, al, bh, bl):
    d = functools.partial(lax.dot_general, dimension_numbers=NT, preferred_element_type=F32)
    return d(ah, bh) + (d(ah, bl) + d(al, bh))


def dynamic(p, size):
    return pl.ds(pl.multiple_of(p * size, size), size)


def chol_stage(p, n, m, block, extra, T, Lh, Ll, U, E, Eh, El, *, before, after_factor, before_rest):
    full = n // 256
    k, half = p // 2, p % 2
    prow = pl.multiple_of(p * 128, 128)
    pcol = pl.ds(prow, 128)
    qcol = pl.ds(pl.multiple_of(prow - half * 128, 128), 128)
    hcol = dynamic(half, 128)

    def update(kk, r, cnt):
        rows = pl.ds(r, cnt)
        x = extra(kk) if isinstance(r, int) and r >= n else block(kk, rows)
        if kk:
            kr = pl.ds(256 * kk, 256)
            x = x - dot3(Lh[rows, :256 * kk], Ll[rows, :256 * kk], Lh[kr, :256 * kk], Ll[kr, :256 * kk])
        T[rows, :] = x

    def half_update(r, cnt):
        rows = pl.ds(r, cnt)
        T[rows, 128:256] = T[rows, 128:256] - dot3(Lh[rows, qcol], Ll[rows, qcol], Lh[pcol, qcol], Ll[pcol, qcol])

    def solve(r, cnt):
        rows = pl.ds(r, cnt)
        th, tl = split(T[rows, hcol])
        x = dot3(th, tl, Eh[...], El[...])
        T[rows, hcol] = x
        xh, xl = split(x)
        Lh[rows, pcol] = xh
        Ll[rows, pcol] = xl

    def rest(body):
        def step(r, _):
            body(pl.multiple_of(r * 256, 256), 256)
            return 0
        lax.fori_loop(k + 1, full, step, 0)
        body(n, m)

    before(p)
    for kk in range(full):
        @pl.when(p == 2 * kk)
        def _():
            update(kk, 256 * kk, 256)

    @pl.when(half == 1)
    def _():
        half_update(prow, 128)

    def su(b, x): U[pl.ds(8 * b, 8), :] = x
    def se(b, x): E[pl.ds(8 * b, 8), :] = x
    factor_block(lambda v: T[pl.ds(pl.multiple_of(prow + 8 * v, 8), 8), hcol], su, se)
    eh, el = split(E[...])
    Eh[...] = eh
    El[...] = el
    after_factor(p)

    @pl.when(half == 0)
    def _():
        solve(pl.multiple_of(prow + 128, 128), 128)
    before_rest(p)
    for kk in range(full):
        @pl.when(p == 2 * kk)
        def _():
            def both(r, cnt):
                update(kk, r, cnt)
                solve(r, cnt)
            rest(both)

    @pl.when(half == 1)
    def _():
        def both(r, cnt):
            half_update(r, cnt)
            solve(r, cnt)
        rest(both)
    T[pl.ds(prow, 128), hcol] = U[...].T


def put_rows(p, n, m, own, row0, T, l_out, c_out):
    hcol, pcol = dynamic(p % 2, 128), dynamic(p, 128)
    c_out[:, pcol] = T[n:n + m, hcol]
    mine = T[pl.ds(pl.multiple_of(row0, own), own), hcol]
    l_out[:, pcol] = jnp.where(p * 128 < row0 + own, mine, 0.0)


def chol_scratch(n, m):
    return [pltpu.VMEM((n + m, 256), F32), pltpu.VMEM((n + m, n), BF), pltpu.VMEM((n + m, n), BF),
            pltpu.VMEM((128, 128), F32), pltpu.VMEM((128, 128), F32),
            pltpu.VMEM((128, 128), BF), pltpu.VMEM((128, 128), BF)]


def nothing(p):
    pass


def parent_kernel(n, m, a_ref, c_ref, l_out, c_out, *scratch):
    T = scratch[0]
    row0 = lax.axis_index("front") * m

    def stage(p, _):
        chol_stage(
            p, n, m,
            lambda kk, rows: a_ref[rows, 256 * kk:256 * kk + 256],
            lambda kk: c_ref[:, 256 * kk:256 * kk + 256],
            *scratch, before=nothing, after_factor=nothing, before_rest=nothing,
        )
        put_rows(p, n, m, m, row0, T, l_out, c_out)
        return 0
    lax.fori_loop(0, n // 128, stage, 0)


def parent_call(n, m):
    return pl.pallas_call(
        functools.partial(parent_kernel, n, m),
        out_shape=[jax.ShapeDtypeStruct((m, n), F32)] * 2,
        in_specs=[pl.BlockSpec(memory_space=pltpu.VMEM)] * 2,
        out_specs=[pl.BlockSpec(memory_space=pltpu.VMEM)] * 2,
        scratch_shapes=chol_scratch(n, m),
        compiler_params=pltpu.CompilerParams(vmem_limit_bytes=40 << 20),
    )


def child_kernel(n, m, land, groups, side, a_ref, c_ref, hit_ref, l_out, c_out, reach,
                 G, LG, own_sem, arrive, first_send, relay_send, land_arrive, land_first, land_relay, *scratch):
    T, Lh, Ll = scratch[0], scratch[1], scratch[2]
    stages, rows_own = n // 128, n // groups
    me = lax.axis_index("front")
    mx, mz = me // side, me % side
    own_parity = (mx + mz) % 2

    def along_z(d):
        return mx * side + (mz + d) % side

    def along_x(d):
        return (mx + d) % side * side + mz

    barrier = pltpu.get_barrier_semaphore()
    for d in range(1, groups):
        pl.semaphore_signal(barrier, inc=1, device_id={"front": (me + d) % groups}, device_id_type=MESH)
    pl.semaphore_wait(barrier, groups - 1)

    def relayed(j):
        if j < side // 2:
            return mx * side + mx % 2 + 2 * j
        return ((mz + 1) % 2 + 2 * (j - side // 2)) * side + mz

    def is_relayed(f):
        even = (f // side + f % side) % 2 == 0
        return ((f // side == mx) & even) | ((f % side == mz) & jnp.logical_not(even))

    def send(src, dst, send_sem, recv_sem, to):
        return pltpu.make_async_remote_copy(src_ref=src, dst_ref=dst, send_sem=send_sem, recv_sem=recv_sem,
                                            device_id={"front": to}, device_id_type=MESH)

    def G_at(k, f):
        return G.at[k, dynamic(f, rows_own), :]

    def own_copy(k):
        return pltpu.make_async_copy(a_ref.at[:, dynamic(k, 256)], G_at(k, me), own_sem.at[k])

    def first(k, d):
        to = jnp.where(own_parity == 0, along_z(d), along_x(d))
        return send(a_ref.at[:, dynamic(k, 256)], G_at(k, me), first_send.at[k, d - 1], arrive.at[k, me], to)

    def relay(k, j, d):
        f = relayed(j)
        to = along_x(d) if j < side // 2 else along_z(d)
        return send(G_at(k, f), G_at(k, f), relay_send.at[k, j, d - 1], arrive.at[k, f], to)

    def arrival(k, f):
        return pltpu.make_async_copy(G_at(k, f), G_at(k, f), arrive.at[k, f])

    def has(k, f):
        return f // 2 >= k

    def start_first(k):
        @pl.when(has(k, me))
        def _():
            for d in range(1, side):
                first(k, d).start()
            own_copy(k).start()

    def start_relay(k):
        for j in range(side):
            f = relayed(j)

            @pl.when(has(k, f))
            def _():
                @pl.when(f != me)
                def _():
                    arrival(k, f).wait()

                @pl.when(f == me)
                def _():
                    own_copy(k).wait()
                for d in range(1, side):
                    relay(k, j, d).start()

    def wait_block(k, f):
        @pl.when((f != me) & jnp.logical_not(is_relayed(f)))
        def _():
            arrival(k, f).wait()

    def wait_blocks(k, lo, hi):
        def step(f, _):
            wait_block(k, f)
            return 0
        lax.fori_loop(lo, hi, step, 0)

    def LG_at(p, f):
        return LG.at[p, dynamic(f, land), :]

    def land_one(p, d):
        to = jnp.where(own_parity == 0, along_z(d), along_x(d))
        return send(LG_at(p, me), LG_at(p, me), land_first.at[d - 1], land_arrive.at[p, me], to)

    def land_two(p, j, d):
        f = relayed(j)
        to = along_x(d) if j < side // 2 else along_z(d)
        return send(LG_at(p, f), LG_at(p, f), land_relay.at[j, d - 1], land_arrive.at[p, f], to)

    def landed(p, f):
        return pltpu.make_async_copy(LG_at(p, f), LG_at(p, f), land_arrive.at[p, f])

    def land_start(p):
        for d in range(1, side):
            @pl.when(p > 0)
            def _():
                land_one(p - 1, d).wait_send()
            land_one(p, d).start()

    def land_pass(p):
        for j in range(side):
            f = relayed(j)

            @pl.when(f != me)
            def _():
                landed(p, f).wait()
            for d in range(1, side):
                @pl.when(p > 0)
                def _():
                    land_two(p - 1, j, d).wait_send()
                land_two(p, j, d).start()

    def land_use(p):
        def step(f, _):
            @pl.when((f != me) & jnp.logical_not(is_relayed(f)))
            def _():
                landed(p, f).wait()
            return 0
        lax.fori_loop(0, groups, step, 0)
        pcol = dynamic(p, 128)
        gh, gl = split(LG[p])
        reach[...] = reach[...] - dot3(Lh[n:n + m, pcol], Ll[n:n + m, pcol], gh, gl)

    for k in range(3):
        start_first(k)
    start_relay(0)
    for k in range(3, n // 256):
        start_first(k)
    start_relay(1)
    reach[...] = jnp.zeros_like(reach)

    def before(p):
        k = p // 2

        @pl.when(p % 2 == 0)
        def _():
            @pl.when(k + 2 < n // 256)
            def _():
                start_relay(k + 2)
            wait_blocks(k, 2 * k, 2 * k + 2)

    def after_factor(p):
        @pl.when(p > 0)
        def _():
            land_pass(p - 1)

    def before_rest(p):
        @pl.when(p % 2 == 0)
        def _():
            wait_blocks(p // 2, p // 2 * 2 + 2, groups)

    def stage(p, _):
        chol_stage(
            p, n, m,
            lambda kk, rows: G[kk, rows, :],
            lambda kk: c_ref[:, 256 * kk:256 * kk + 256],
            *scratch, before=before, after_factor=after_factor, before_rest=before_rest,
        )
        pcol = dynamic(p, 128)
        nn = functools.partial(jnp.dot, preferred_element_type=F32)
        LG[p, dynamic(me, land), :] = nn(hit_ref[...], Lh[n:n + m, pcol]) + nn(hit_ref[...], Ll[n:n + m, pcol])
        put_rows(p, n, m, rows_own, me * rows_own, T, l_out, c_out)

        @pl.when(p >= 3)
        def _():
            land_use(p - 3)
        land_start(p)
        return 0
    lax.fori_loop(0, stages, stage, 0)
    land_use(stages - 3)
    land_pass(stages - 1)
    land_use(stages - 2)
    land_use(stages - 1)
    for d in range(1, side):
        land_one(stages - 1, d).wait_send()
        for j in range(side):
            land_two(stages - 1, j, d).wait_send()

    def drain(k, _):
        @pl.when(has(k, me))
        def _():
            for d in range(1, side):
                first(k, d).wait_send()
        for j in range(side):
            @pl.when(has(k, relayed(j)))
            def _():
                for d in range(1, side):
                    relay(k, j, d).wait_send()
        return 0
    lax.fori_loop(0, n // 256, drain, 0)


def child_call(n, m, land, groups, side):
    dma = pltpu.SemaphoreType.DMA
    stages = n // 128
    vmem = pl.BlockSpec(memory_space=pltpu.VMEM)
    return pl.pallas_call(
        functools.partial(child_kernel, n, m, land, groups, side),
        out_shape=[jax.ShapeDtypeStruct((n // groups, n), F32), jax.ShapeDtypeStruct((m, n), F32),
                   jax.ShapeDtypeStruct((m, land * groups), F32)],
        in_specs=[pl.BlockSpec(memory_space=pl.ANY), vmem, vmem],
        out_specs=[vmem] * 3,
        scratch_shapes=[
            pltpu.VMEM((n // 256, n, 256), F32), pltpu.VMEM((stages, land * groups, 128), F32),
            dma((n // 256,)), dma((n // 256, groups)), dma((n // 256, side - 1)), dma((n // 256, side, side - 1)),
            dma((stages, groups)), dma((side - 1,)), dma((side, side - 1)),
        ] + chol_scratch(n, m),
        compiler_params=pltpu.CompilerParams(vmem_limit_bytes=62 << 20, collective_id=0, has_side_effects=True),
    )


def sent_and_summed(array, axis):
    pieces = array.reshape(lax.axis_size(axis), -1, array.shape[1])
    arrived = lax.all_to_all(pieces, axis, split_axis=0, concat_axis=0, tiled=True)
    return arrived.sum(axis=0)


def on_device(child_pivot, child_coupling, parent_arrow, row_map, block_pattern):
    own_rows = child_pivot[0]
    parent_index = row_map[0]
    row_count, pivot_count = own_rows.shape
    parent_count, pivots = parent_arrow.shape
    front_index = lax.axis_index("front")
    front_groups = lax.axis_size("front")
    slot_index = (
        parent_index // parent_count // front_groups * parent_count + parent_index % parent_count
    )
    spread_rows = lax.axis_size("bulk") * parent_count
    routing = (slot_index[:, None] == jnp.arange(spread_rows)[None, :]).astype(F32)
    hits = routing[:, :parent_count].T.astype(BF)
    lower_rows, coupling, reached = child_call(pivot_count, row_count, parent_count, front_groups, 4)(
        own_rows, child_coupling[0], hits
    )
    routed = jnp.dot(routing.T, reached, precision=HIGHEST_PRECISION)
    device_index = lax.axis_index("bulk") * front_groups + front_index
    first_row = device_index * parent_count
    block_rows = (first_row + jnp.arange(parent_count)) // BLOCK
    picker = (block_rows[:, None] == jnp.arange(block_pattern.shape[0])[None, :]).astype(F32)
    row_mask = jnp.dot(picker, block_pattern.astype(F32), precision=HIGHEST_PRECISION)
    masked = parent_arrow * jnp.repeat(row_mask, BLOCK, axis=1)
    top = routed[:parent_count] + jnp.where(lax.axis_index("bulk") == 0, masked, 0.0)
    top = lax.psum(top, "bulk")
    pivot_block = lax.all_gather(top, "front", axis=0, tiled=True)
    assembled = masked + sent_and_summed(routed, "bulk")
    factor_rows, solved = parent_call(pivots, parent_count)(pivot_block, assembled)
    parent_rows = jnp.where(first_row < pivots, factor_rows, solved)
    return (lower_rows[None], coupling[None], parent_rows)


def solution(mesh):
    placed = (
        P("bulk", "front", None),
        P("bulk", "front", None),
        P(("bulk", "front"), None),
        P("bulk", "front"),
        P(),
    )
    return jax.shard_map(
        on_device,
        mesh=mesh,
        in_specs=placed,
        out_specs=(P("bulk", "front", None), P("bulk", "front", None), P(("bulk", "front"), None)),
        check_vma=False,
    )
```

```python
import functools

import jax
import jax.numpy as jnp
from jax import lax
from jax.experimental import pallas as pl
from jax.experimental.pallas import tpu as pltpu
from jax.sharding import PartitionSpec as P

BLOCK = 128
F32, BF = jnp.float32, jnp.bfloat16
NT = (((1,), (1,)), ((), ()))
MESH = pl.DeviceIdType.MESH
HIGHEST_PRECISION = lax.Precision.HIGHEST


def factor_block(load_row, store_u, store_e, n=128, sb=8):
    nb = n // sb
    W = [load_row(v) for v in range(nb)]
    lane = lax.broadcasted_iota(jnp.int32, (sb, n), 1)
    sub = lax.broadcasted_iota(jnp.int32, (sb, n), 0)
    for b in range(nb):
        base = b * sb
        inblk = (lane >= base) & (lane < base + sb)
        R = W[b]
        S = [jnp.broadcast_to(R[:, base + j:base + j + 1], (sb, n)) for j in range(sb)]
        F = {}
        for j in range(sb):
            for i in range(j, sb):
                F[i, j] = jnp.broadcast_to(S[j][i:i + 1, :], (sb, n))
        rinv = []
        for j in range(sb):
            r = lax.rsqrt(F[j, j])
            rinv.append(r)
            for i in range(j, sb):
                F[i, j] = F[i, j] * r
            for c in range(j + 1, sb):
                for i in range(c, sb):
                    F[i, c] = F[i, c] - F[i, j] * F[c, j]
        RI = jnp.where(inblk, (lane - base == sub).astype(jnp.float32), R)
        u = []
        for j in range(sb):
            t = jnp.broadcast_to(RI[j:j + 1, :], (sb, n))
            for m in range(j):
                t = t - F[j, m] * u[m]
            u.append(t * rinv[j])
        e = u[0]
        for j in range(1, sb):
            e = jnp.where(sub == j, u[j], e)
        store_e(b, jnp.where(lane < base + sb, e, 0.0))
        d = jnp.zeros((sb, n), jnp.float32)
        for j in range(sb):
            for c in range(j, sb):
                d = jnp.where((sub == j) & (lane == base + c), F[c, j], d)
        store_u(b, jnp.where(inblk, d, jnp.where(lane < base, 0.0, e)))
        for v in range(b + 1, nb):
            C = []
            acc = jnp.where(inblk, 0.0, W[v])
            for j in range(sb):
                c = jnp.broadcast_to(W[v][:, base + j:base + j + 1], (sb, n))
                for m in range(j):
                    c = c - C[m] * F[j, m]
                c = c * rinv[j]
                C.append(c)
                acc = acc - c * u[j]
            W[v] = acc


def split(x):
    hi = x.astype(BF)
    return hi, (x - hi.astype(F32)).astype(BF)

def dot3(ah, al, bh, bl):
    d = functools.partial(lax.dot_general, dimension_numbers=NT, preferred_element_type=F32)
    return d(ah, bh) + (d(ah, bl) + d(al, bh))


def dynamic(p, size):
    return pl.ds(pl.multiple_of(p * size, size), size)


def chol_stage(p, n, m, block, extra, T, Lh, Ll, U, E, Eh, El, *, before, after_factor, before_rest):
    full = n // 256
    k, half = p // 2, p % 2
    prow = pl.multiple_of(p * 128, 128)
    pcol = pl.ds(prow, 128)
    qcol = pl.ds(pl.multiple_of(prow - half * 128, 128), 128)
    hcol = dynamic(half, 128)

    def update(kk, r, cnt):
        rows = pl.ds(r, cnt)
        x = extra(kk) if isinstance(r, int) and r >= n else block(kk, rows)
        if kk:
            kr = pl.ds(256 * kk, 256)
            x = x - dot3(Lh[rows, :256 * kk], Ll[rows, :256 * kk], Lh[kr, :256 * kk], Ll[kr, :256 * kk])
        T[rows, :] = x

    def half_update(r, cnt):
        rows = pl.ds(r, cnt)
        T[rows, 128:256] = T[rows, 128:256] - dot3(Lh[rows, qcol], Ll[rows, qcol], Lh[pcol, qcol], Ll[pcol, qcol])

    def solve(r, cnt):
        rows = pl.ds(r, cnt)
        th, tl = split(T[rows, hcol])
        x = dot3(th, tl, Eh[...], El[...])
        T[rows, hcol] = x
        xh, xl = split(x)
        Lh[rows, pcol] = xh
        Ll[rows, pcol] = xl

    def rest(body):
        def step(r, _):
            body(pl.multiple_of(r * 256, 256), 256)
            return 0
        lax.fori_loop(k + 1, full, step, 0)
        if m:
            body(n, m)

    before(p)
    for kk in range(full):
        @pl.when(p == 2 * kk)
        def _():
            update(kk, 256 * kk, 256)

    @pl.when(half == 1)
    def _():
        half_update(prow, 128)

    def su(b, x): U[pl.ds(8 * b, 8), :] = x
    def se(b, x): E[pl.ds(8 * b, 8), :] = x
    factor_block(lambda v: T[pl.ds(pl.multiple_of(prow + 8 * v, 8), 8), hcol], su, se)
    eh, el = split(E[...])
    Eh[...] = eh
    El[...] = el
    after_factor(p)

    @pl.when(half == 0)
    def _():
        solve(pl.multiple_of(prow + 128, 128), 128)
    before_rest(p)
    for kk in range(full):
        @pl.when(p == 2 * kk)
        def _():
            def both(r, cnt):
                update(kk, r, cnt)
                solve(r, cnt)
            rest(both)

    @pl.when(half == 1)
    def _():
        def both(r, cnt):
            half_update(r, cnt)
            solve(r, cnt)
        rest(both)
    T[pl.ds(prow, 128), hcol] = U[...].T


def put_rows(p, n, m, own, row0, T, l_out, c_out):
    hcol, pcol = dynamic(p % 2, 128), dynamic(p, 128)
    c_out[:, pcol] = T[n:n + m, hcol]
    mine = T[pl.ds(pl.multiple_of(row0, own), own), hcol]
    l_out[:, pcol] = jnp.where(p * 128 < row0 + own, mine, 0.0)


def chol_scratch(n, m):
    return [pltpu.VMEM((n + m, 256), F32), pltpu.VMEM((n + m, n), BF), pltpu.VMEM((n + m, n), BF),
            pltpu.VMEM((128, 128), F32), pltpu.VMEM((128, 128), F32),
            pltpu.VMEM((128, 128), BF), pltpu.VMEM((128, 128), BF)]


def nothing(p):
    pass


def remote(src, dst, send_sem, recv_sem, to):
    return pltpu.make_async_remote_copy(src_ref=src, dst_ref=dst, send_sem=send_sem, recv_sem=recv_sem,
                                        device_id=to, device_id_type=MESH)


def meet(axes):
    barrier = pltpu.get_barrier_semaphore()
    count = 0
    for axis, size in axes:
        here = lax.axis_index(axis)
        for d in range(1, size):
            pl.semaphore_signal(barrier, inc=1, device_id={axis: (here + d) % size}, device_id_type=MESH)
        count += size - 1
    pl.semaphore_wait(barrier, count)


class Square:
    def __init__(self, at, arrive, sems, has, own_ready, once):
        self.at, self.arrive, self.sems, self.has, self.own_ready, self.once = at, arrive, sems, has, own_ready, once
        me = lax.axis_index("front")
        self.me, self.x, self.z = me, me // 4, me % 4
        self.parity = (self.x + self.z) % 2

    def near(self, axis, d):
        along_z = self.x * 4 + (self.z + d) % 4
        along_x = (self.x + d) % 4 * 4 + self.z
        if isinstance(axis, int):
            return along_x if axis else along_z
        return jnp.where(axis == 0, along_z, along_x)

    def copy(self, k, f, part, phase, slot, to, src=None):
        s = 0 if self.once else k
        dst = self.at(k, f, part)
        return remote(dst if src is None else src, dst, self.sems[phase].at[s, slot], self.arrive.at[k, f], {"front": to})

    def arrival(self, k, f):
        return pltpu.make_async_copy(self.at(k, f, None), self.at(k, f, None), self.arrive.at[k, f])

    def plan(self, phase):
        x, z = self.x, self.z
        if phase == 0:
            return [(self.me, None, 0, self.near(self.parity, 1)), (self.me, None, 1, self.near(self.parity, 3))]
        if phase == 1:
            r = 1 - self.parity
            return [(self.near(r, 3), 0, 0, self.near(r, 1)), (self.near(r, 1), 1, 1, self.near(r, 3))]
        out = []
        if phase == 2:
            for j in range(2):
                f = x * 4 + x % 2 + 2 * j
                g = ((z + 1) % 2 + 2 * j) * 4 + z
                for d, i in ((1, 0), (3, 1)):
                    out.append((f, None, 4 * j + i, self.near(1, d)))
                for d, i in ((1, 2), (3, 3)):
                    out.append((g, None, 4 * j + i, self.near(0, d)))
            return out
        for j in range(2):
            for d, part in ((3, 0), (1, 1)):
                back = 4 - d
                xs, zs = (x + d) % 4, (z + d) % 4
                out.append((xs * 4 + xs % 2 + 2 * j, part, 4 * j + part, self.near(1, back)))
                out.append((((zs + 1) % 2 + 2 * j) * 4 + zs, part, 4 * j + 2 + part, self.near(0, back)))
        return out

    def start(self, phase, k, src=None):
        seen = None
        for f, part, slot, to in self.plan(phase):
            new = f is not seen
            seen = f

            @pl.when(self.has(k, f))
            def _():
                if new and phase in (1, 3):
                    self.arrival(k, f).wait()
                if new and phase == 2:
                    @pl.when(f == self.me)
                    def _():
                        self.own_ready(k)

                    @pl.when((f == self.near(0, 2)) | (f == self.near(1, 2)))
                    def _():
                        self.arrival(k, f).wait()
                if self.once:
                    @pl.when(k > 0)
                    def _():
                        self.copy(k - 1, f, part, phase, slot, to, src).wait_send()
                self.copy(k, f, part, phase, slot, to, src).start()

    def finish(self, k, lo, hi):
        for j in range(2):
            xs, zs = (self.x + 2) % 4, (self.z + 2) % 4
            for f in (xs * 4 + xs % 2 + 2 * j, ((zs + 1) % 2 + 2 * j) * 4 + zs):
                @pl.when(self.has(k, f) & (f >= lo) & (f < hi))
                def _():
                    self.arrival(k, f).wait()

    def prologue(self, first):
        first(0)
        self.start(1, 0)
        first(1)
        self.start(2, 0)
        self.start(1, 1)
        first(2)
        self.start(3, 0)
        self.start(2, 1)
        self.start(1, 2)
        first(3)

    def ahead(self, s, wide, first):
        j = s // 3

        @pl.when(s % 3 == 0)
        def _():
            @pl.when(j + 2 < wide)
            def _():
                self.start(2, j + 2)

            @pl.when(j + 3 < wide)
            def _():
                self.start(1, j + 3)

            @pl.when(j + 4 < wide)
            def _():
                first(j + 4)

        @pl.when((s % 3 == 1) & (j + 1 < wide))
        def _():
            self.start(3, j + 1)

    def drain(self, k, src=None):
        for phase in range(4):
            for f, part, slot, to in self.plan(phase):
                @pl.when(self.has(k, f))
                def _():
                    self.copy(k, f, part, phase, slot, to, src if phase == 0 else None).wait_send()


def square_sems(n):
    return [pltpu.SemaphoreType.DMA((n, c)) for c in (2, 2, 8, 8)]


def child_kernel(n, m, land, groups, a_ref, c_ref, hit_ref, l_out, c_out, reach, G, LG, own_sem, arrive, land_arrive, *more):
    sems, land_sems, scratch = more[:4], more[4:8], more[8:]
    T, Lh, Ll = scratch[0], scratch[1], scratch[2]
    stages, rows_own, wide = n // 128, n // groups, n // 256
    me = lax.axis_index("front")
    meet((("front", groups),))

    def part_of(ref, k, f, size, part):
        if part is None:
            return ref.at[k, dynamic(f, size), :]
        return ref.at[k, dynamic(2 * f + part, size // 2), :]

    def own_copy(k):
        return pltpu.make_async_copy(a_ref.at[:, dynamic(k, 256)], G.at[k, dynamic(me, rows_own), :], own_sem.at[k])

    def has(k, f):
        return f // 2 >= k
    rows = Square(lambda k, f, part: part_of(G, k, f, rows_own, part), arrive, sems, has, lambda k: own_copy(k).wait(), False)
    lands = Square(lambda k, f, part: part_of(LG, k, f, land, part), land_arrive, land_sems,
                   lambda k, f: f >= 0, nothing, True)

    def first(k):
        rows.start(0, k, a_ref.at[:, dynamic(k, 256)])

        @pl.when(has(k, me))
        def _():
            own_copy(k).start()

    def land_use(p):
        lands.finish(p, 0, groups)
        pcol = dynamic(p, 128)
        gh, gl = split(LG[p])
        reach[...] = reach[...] - dot3(Lh[n:n + m, pcol], Ll[n:n + m, pcol], gh, gl)

    def catch_up(p, late, long, short, body):
        def upto(q):
            return jnp.where(q >= late, q - short, q - long)

        def step(q, _):
            body(q)
            return 0
        lax.fori_loop(jnp.maximum(upto(p - 1) + 1, 0), jnp.maximum(upto(p) + 1, 0), step, 0)

    rows.prologue(first)
    reach[...] = jnp.zeros_like(reach)

    def before(p):
        @pl.when(p % 2 == 0)
        def _():
            rows.finish(p // 2, p, p + 2)

    def after_factor(p):
        rows.ahead(2 * p, wide, first)
        catch_up(p, 11, 2, 1, lambda q: lands.start(1, q))
        catch_up(p, 12, 5, 2, lambda q: lands.start(3, q))

    def before_rest(p):
        @pl.when(p % 2 == 0)
        def _():
            rows.finish(p // 2, p + 2, groups)

    def stage(p, _):
        chol_stage(
            p, n, m,
            lambda kk, rows: G[kk, rows, :],
            lambda kk: c_ref[:, 256 * kk:256 * kk + 256],
            *scratch, before=before, after_factor=after_factor, before_rest=before_rest,
        )
        pcol = dynamic(p, 128)
        nn = functools.partial(jnp.dot, preferred_element_type=F32)
        LG[p, dynamic(me, land), :] = nn(hit_ref[...], Lh[n:n + m, pcol]) + nn(hit_ref[...], Ll[n:n + m, pcol])
        put_rows(p, n, m, rows_own, me * rows_own, T, l_out, c_out)

        rows.ahead(2 * p + 1, wide, first)
        catch_up(p, 11, 3, 1, lambda q: lands.start(2, q))
        catch_up(p, 12, 6, 3, land_use)
        lands.start(0, p)
        return 0
    lax.fori_loop(0, stages, stage, 0)
    last = stages - 1
    lands.start(3, last - 1)
    lands.start(1, last)
    land_use(last - 2)
    lands.start(2, last)
    land_use(last - 1)
    lands.start(3, last)
    land_use(last)
    lands.drain(last)

    def drain(k, _):
        rows.drain(k, a_ref.at[:, dynamic(k, 256)])
        return 0
    lax.fori_loop(0, wide, drain, 0)


def child_call(n, m, land, groups, side):
    dma = pltpu.SemaphoreType.DMA
    stages = n // 128
    vmem = pl.BlockSpec(memory_space=pltpu.VMEM)
    return pl.pallas_call(
        functools.partial(child_kernel, n, m, land, groups),
        out_shape=[jax.ShapeDtypeStruct((n // groups, n), F32), jax.ShapeDtypeStruct((m, n), F32),
                   jax.ShapeDtypeStruct((m, land * groups), F32)],
        in_specs=[pl.BlockSpec(memory_space=pl.ANY), vmem, vmem],
        out_specs=[vmem] * 3,
        scratch_shapes=[
            pltpu.VMEM((n // 256, n, 256), F32), pltpu.VMEM((stages, land * groups, 128), F32),
            dma((n // 256,)), dma((n // 256, groups)), dma((stages, groups)),
        ] + square_sems(n // 256) + square_sems(1) + chol_scratch(n, m),
        compiler_params=pltpu.CompilerParams(vmem_limit_bytes=62 << 20, collective_id=0, has_side_effects=True),
    )


def parent_kernel(n, m, groups, bulks, reach, route, masked, out, PV, TP, RS, SB, RB, XH, XL, EH, EL,
                  scatter_send, scatter_come, gather_send, gather_come, spread_send, spread_come, arrive, *more):
    sems, scratch = more[:4], more[4:]
    T, Lh, Ll, U, E, Eh, El = scratch
    wide, full = n // 256, n // 128
    me, here = lax.axis_index("front"), lax.axis_index("bulk")
    meet((("front", groups), ("bulk", bulks)))
    nn = functools.partial(jnp.dot, preferred_element_type=F32)
    rh, rl = split(reach[...])

    def slot(b):
        r = route[b * m:(b + 1) * m, :]
        return nn(r, rh) + nn(r, rl)

    def other(d):
        return (here + d) % bulks

    def needed(j):
        return j // 2 <= me // 4

    def scatter(d):
        j = other(d)
        return remote(TP.at[j], RS.at[here], scatter_send.at[d - 1], scatter_come.at[here], {"bulk": j})

    def scattered(b):
        return pltpu.make_async_copy(RS.at[b], RS.at[b], scatter_come.at[b])

    def piece(j):
        return PV.at[j // 2, dynamic(me, m), dynamic(j % 2, 128)]

    def gather(d):
        return remote(piece(here), piece(here), gather_send.at[d - 1], gather_come.at[here], {"bulk": other(d)})

    def spread(d):
        b = other(d)
        return remote(SB.at[b], RB.at[here], spread_send.at[d - 1], spread_come.at[here], {"bulk": b})

    def spreaded(b):
        return pltpu.make_async_copy(RB.at[b], RB.at[b], spread_come.at[b])

    top = slot(0) + jnp.where(here == 0, masked[...], 0.0)
    for j in range(full):
        TP[j] = top[:, 128 * j:128 * j + 128]
    for d in range(1, bulks):
        @pl.when(needed(other(d)))
        def _():
            scatter(d).start()
    for b in range(1, bulks):
        SB[b] = slot(b)

    @pl.when(needed(here))
    def _():
        RS[here] = TP[here]
        for d in range(1, bulks):
            scattered(other(d)).wait()
        total = RS[0]
        for b in range(1, bulks):
            total = total + RS[b]
        PV[here // 2, dynamic(me, m), dynamic(here % 2, 128)] = total
        for d in range(1, bulks):
            gather(d).start()
    for d in range(1, bulks):
        j = other(d)

        @pl.when(needed(j))
        def _():
            pltpu.make_async_copy(piece(j), piece(j), gather_come.at[j]).wait()

    def part_at(k, f, part):
        if part is None:
            return PV.at[k, dynamic(f, m), :]
        return PV.at[k, dynamic(2 * f + part, m // 2), :]
    rows = Square(part_at, arrive, sems, lambda k, f: f // 4 >= k, nothing, False)

    def first(k):
        rows.start(0, k)
    first(0)
    for d in range(1, bulks):
        @pl.when(other(d) != 0)
        def _():
            spread(d).start()
    rows.start(1, 0)
    first(1)
    rows.start(2, 0)
    rows.start(1, 1)
    first(2)
    rows.start(3, 0)
    rows.start(2, 1)
    rows.start(1, 2)
    first(3)

    def before(p):
        @pl.when(p % 2 == 0)
        def _():
            rows.finish(p // 2, 2 * p, 2 * p + 4)

    def before_rest(p):
        @pl.when(p % 2 == 0)
        def _():
            rows.finish(p // 2, 2 * p + 4, groups)

    def stage(p, _):
        chol_stage(p, n, 0, lambda kk, r: PV[kk, r, :], None, *scratch, before=before,
                   after_factor=lambda p: rows.ahead(2 * p, wide, first), before_rest=before_rest)
        EH[p] = Eh[...]
        EL[p] = El[...]
        mine = T[dynamic(me, m), dynamic(p % 2, 128)]
        out[:, dynamic(p, 128)] = jnp.where(p * 128 < (me + 1) * m, mine, 0.0)
        rows.ahead(2 * p + 1, wide, first)
        return 0
    lax.fori_loop(0, full, stage, 0)

    @pl.when(here != 0)
    def _():
        for d in range(1, bulks):
            spreaded(other(d)).wait()
        RB[here] = SB[here]
        x = masked[...]
        for b in range(bulks):
            x = x + RB[b]
        for p in range(full):
            cols = slice(128 * p, 128 * p + 128)
            y = x[:, cols]
            if p:
                y = y - dot3(XH[:, :128 * p], XL[:, :128 * p], Lh[cols, :128 * p], Ll[cols, :128 * p])
            yh, yl = split(y)
            y = dot3(yh, yl, EH[p], EL[p])
            out[:, cols] = y
            yh, yl = split(y)
            XH[:, cols] = yh
            XL[:, cols] = yl
    for d in range(1, bulks):
        @pl.when(needed(other(d)))
        def _():
            scatter(d).wait_send()

        @pl.when(needed(here))
        def _():
            gather(d).wait_send()

        @pl.when(other(d) != 0)
        def _():
            spread(d).wait_send()

    def drain(k, _):
        rows.drain(k)
        return 0
    lax.fori_loop(0, wide, drain, 0)


def parent_call(n, m, groups, bulks):
    dma = pltpu.SemaphoreType.DMA
    vmem = pl.BlockSpec(memory_space=pltpu.VMEM)
    full, wide = n // 128, n // 256
    return pl.pallas_call(
        functools.partial(parent_kernel, n, m, groups, bulks),
        out_shape=jax.ShapeDtypeStruct((m, n), F32),
        in_specs=[vmem] * 3,
        out_specs=vmem,
        scratch_shapes=[
            pltpu.VMEM((wide, n, 256), F32), pltpu.VMEM((full, m, 128), F32), pltpu.VMEM((bulks, m, 128), F32),
            pltpu.VMEM((bulks, m, n), F32), pltpu.VMEM((bulks, m, n), F32), pltpu.VMEM((m, n), BF), pltpu.VMEM((m, n), BF),
            pltpu.VMEM((full, 128, 128), BF), pltpu.VMEM((full, 128, 128), BF),
            dma((bulks - 1,)), dma((bulks,)), dma((bulks - 1,)), dma((bulks,)), dma((bulks - 1,)), dma((bulks,)),
            dma((wide, groups)),
        ] + square_sems(wide) + chol_scratch(n, 0),
        compiler_params=pltpu.CompilerParams(vmem_limit_bytes=40 << 20, collective_id=1, has_side_effects=True),
    )


def on_device(child_pivot, child_coupling, parent_arrow, row_map, block_pattern):
    own_rows = child_pivot[0]
    parent_index = row_map[0]
    row_count, pivot_count = own_rows.shape
    parent_count, pivots = parent_arrow.shape
    front_index = lax.axis_index("front")
    front_groups = lax.axis_size("front")
    slot_index = (
        parent_index // parent_count // front_groups * parent_count + parent_index % parent_count
    )
    spread_rows = lax.axis_size("bulk") * parent_count
    routing = (jnp.arange(spread_rows)[:, None] == slot_index[None, :]).astype(BF)
    lower_rows, coupling, reached = child_call(pivot_count, row_count, parent_count, front_groups, 4)(
        own_rows, child_coupling[0], routing[:parent_count]
    )
    device_index = lax.axis_index("bulk") * front_groups + front_index
    first_row = device_index * parent_count
    block_rows = (first_row + jnp.arange(parent_count)) // BLOCK
    picker = (block_rows[:, None] == jnp.arange(block_pattern.shape[0])[None, :]).astype(F32)
    row_mask = jnp.dot(picker, block_pattern.astype(F32), precision=HIGHEST_PRECISION)
    masked = parent_arrow * jnp.repeat(row_mask, BLOCK, axis=1)
    parent_rows = parent_call(pivots, parent_count, front_groups, lax.axis_size("bulk"))(reached, routing, masked)
    return (lower_rows[None], coupling[None], parent_rows)


def solution(mesh):
    placed = (
        P("bulk", "front", None),
        P("bulk", "front", None),
        P(("bulk", "front"), None),
        P("bulk", "front"),
        P(),
    )
    return jax.shard_map(
        on_device,
        mesh=mesh,
        in_specs=placed,
        out_specs=(P("bulk", "front", None), P("bulk", "front", None), P(("bulk", "front"), None)),
        check_vma=False,
    )
```

```python
import functools

import jax
import jax.numpy as jnp
from jax import lax
from jax.experimental import pallas as pl
from jax.experimental.pallas import tpu as pltpu
from jax.sharding import PartitionSpec as P

BLOCK = 128
F32, BF = jnp.float32, jnp.bfloat16
NT = (((1,), (1,)), ((), ()))
MESH = pl.DeviceIdType.MESH
HIGHEST_PRECISION = lax.Precision.HIGHEST


def factor_block(load_row, store_u, store_e, n=128, sb=8):
    nb = n // sb
    W = [load_row(v) for v in range(nb)]
    lane = lax.broadcasted_iota(jnp.int32, (sb, n), 1)
    sub = lax.broadcasted_iota(jnp.int32, (sb, n), 0)
    for b in range(nb):
        base = b * sb
        inblk = (lane >= base) & (lane < base + sb)
        R = W[b]
        S = [jnp.broadcast_to(R[:, base + j:base + j + 1], (sb, n)) for j in range(sb)]
        F = {}
        for j in range(sb):
            for i in range(j, sb):
                F[i, j] = jnp.broadcast_to(S[j][i:i + 1, :], (sb, n))
        rinv = []
        for j in range(sb):
            r = lax.rsqrt(F[j, j])
            rinv.append(r)
            for i in range(j, sb):
                F[i, j] = F[i, j] * r
            for c in range(j + 1, sb):
                for i in range(c, sb):
                    F[i, c] = F[i, c] - F[i, j] * F[c, j]
        RI = jnp.where(inblk, (lane - base == sub).astype(jnp.float32), R)
        u = []
        for j in range(sb):
            t = jnp.broadcast_to(RI[j:j + 1, :], (sb, n))
            for m in range(j):
                t = t - F[j, m] * u[m]
            u.append(t * rinv[j])
        e = u[0]
        for j in range(1, sb):
            e = jnp.where(sub == j, u[j], e)
        store_e(b, jnp.where(lane < base + sb, e, 0.0))
        d = jnp.zeros((sb, n), jnp.float32)
        for j in range(sb):
            for c in range(j, sb):
                d = jnp.where((sub == j) & (lane == base + c), F[c, j], d)
        store_u(b, jnp.where(inblk, d, jnp.where(lane < base, 0.0, e)))
        for v in range(b + 1, nb):
            C = []
            acc = jnp.where(inblk, 0.0, W[v])
            for j in range(sb):
                c = jnp.broadcast_to(W[v][:, base + j:base + j + 1], (sb, n))
                for m in range(j):
                    c = c - C[m] * F[j, m]
                c = c * rinv[j]
                C.append(c)
                acc = acc - c * u[j]
            W[v] = acc


def split(x):
    hi = x.astype(BF)
    return hi, (x - hi.astype(F32)).astype(BF)

def dot3(ah, al, bh, bl):
    d = functools.partial(lax.dot_general, dimension_numbers=NT, preferred_element_type=F32)
    return d(ah, bh) + (d(ah, bl) + d(al, bh))


def dynamic(p, size):
    return pl.ds(pl.multiple_of(p * size, size), size)


def stack(ref, bh, bl):
    ref[0:128, 0:128] = bh
    ref[0:128, 128:256] = bh
    ref[128:256, 0:128] = bl
    ref[128:256, 128:256] = jnp.zeros_like(bl)


def dot_stacked(ah, al, ref):
    y = lax.dot_general(jnp.concatenate([ah, al], axis=1), ref[...], NT, preferred_element_type=F32)
    return y[:, :128] + y[:, 128:]


def chol_stage(p, n, m, block, extra, T, Lh, Ll, U, E, ES, LS, *, before, after_factor, before_rest):
    full = n // 256
    k, half = p // 2, p % 2
    prow = pl.multiple_of(p * 128, 128)
    pcol = pl.ds(prow, 128)
    qcol = pl.ds(pl.multiple_of(prow - half * 128, 128), 128)
    hcol = dynamic(half, 128)

    def update(kk, r, cnt):
        rows = pl.ds(r, cnt)
        x = extra(kk) if isinstance(r, int) and r >= n else block(kk, rows)
        if kk:
            kr = pl.ds(256 * kk, 256)
            x = x - dot3(Lh[rows, :256 * kk], Ll[rows, :256 * kk], Lh[kr, :256 * kk], Ll[kr, :256 * kk])
        T[rows, :] = x

    def half_update(r, cnt):
        rows = pl.ds(r, cnt)
        T[rows, 128:256] = T[rows, 128:256] - dot_stacked(Lh[rows, qcol], Ll[rows, qcol], LS)

    def solve(r, cnt):
        rows = pl.ds(r, cnt)
        th, tl = split(T[rows, hcol])
        x = dot_stacked(th, tl, ES)
        T[rows, hcol] = x
        xh, xl = split(x)
        Lh[rows, pcol] = xh
        Ll[rows, pcol] = xl

    def rest(first, body):
        count = full - first

        def step(i, _):
            body(pl.multiple_of(first * 256 + i * 512, 256), 512)
            return 0
        lax.fori_loop(0, count // 2, step, 0)
        if not isinstance(first, int):
            pl.when(count % 2 == 1)(lambda: body(n - 256, 256))
        elif count % 2:
            body(n - 256, 256)
        if m:
            body(n, m)

    before(p)
    for kk in range(full):
        @pl.when(p == 2 * kk)
        def _():
            update(kk, 256 * kk, 256)

    @pl.when(half == 1)
    def _():
        stack(LS, Lh[pcol, qcol], Ll[pcol, qcol])
        half_update(prow, 128)

    def su(b, x): U[pl.ds(8 * b, 8), :] = x
    def se(b, x): E[pl.ds(8 * b, 8), :] = x
    factor_block(lambda v: T[pl.ds(pl.multiple_of(prow + 8 * v, 8), 8), hcol], su, se)
    stack(ES, *split(E[...]))
    after_factor(p)

    @pl.when(half == 0)
    def _():
        solve(pl.multiple_of(prow + 128, 128), 128)
    before_rest(p)
    for kk in range(full):
        @pl.when(p == 2 * kk)
        def _():
            def both(r, cnt):
                update(kk, r, cnt)
                solve(r, cnt)
            rest(kk + 1, both)

    @pl.when(half == 1)
    def _():
        def both(r, cnt):
            half_update(r, cnt)
            solve(r, cnt)
        rest(k + 1, both)
    T[pl.ds(prow, 128), hcol] = U[...].T


def put_rows(p, n, m, own, row0, T, l_out, c_out):
    hcol, pcol = dynamic(p % 2, 128), dynamic(p, 128)
    c_out[:, pcol] = T[n:n + m, hcol]
    mine = T[pl.ds(pl.multiple_of(row0, own), own), hcol]
    l_out[:, pcol] = jnp.where(p * 128 < row0 + own, mine, 0.0)


def chol_scratch(n, m):
    return [pltpu.VMEM((n + m, 256), F32), pltpu.VMEM((n + m, n), BF), pltpu.VMEM((n + m, n), BF),
            pltpu.VMEM((128, 128), F32), pltpu.VMEM((128, 128), F32),
            pltpu.VMEM((256, 256), BF), pltpu.VMEM((256, 256), BF)]


def nothing(p):
    pass


def remote(src, dst, send_sem, recv_sem, to):
    return pltpu.make_async_remote_copy(src_ref=src, dst_ref=dst, send_sem=send_sem, recv_sem=recv_sem,
                                        device_id=to, device_id_type=MESH)


def meet(axes):
    barrier = pltpu.get_barrier_semaphore()
    count = 0
    for axis, size in axes:
        here = lax.axis_index(axis)
        for d in range(1, size):
            pl.semaphore_signal(barrier, inc=1, device_id={axis: (here + d) % size}, device_id_type=MESH)
        count += size - 1
    pl.semaphore_wait(barrier, count)


class Square:
    def __init__(self, at, arrive, sems, has, own_ready, once):
        self.at, self.arrive, self.sems, self.has, self.own_ready, self.once = at, arrive, sems, has, own_ready, once
        me = lax.axis_index("front")
        self.me, self.x, self.z = me, me // 4, me % 4
        self.parity = (self.x + self.z) % 2
        self.plans = [self.plan(phase) for phase in range(4)]
        self.opposite = self.near(0, 2), self.near(1, 2)
        xs, zs = (self.x + 2) % 4, (self.z + 2) % 4
        self.final = [f for j in range(2) for f in (xs * 4 + xs % 2 + 2 * j, ((zs + 1) % 2 + 2 * j) * 4 + zs)]

    def near(self, axis, d):
        along_z = self.x * 4 + (self.z + d) % 4
        along_x = (self.x + d) % 4 * 4 + self.z
        if isinstance(axis, int):
            return along_x if axis else along_z
        return jnp.where(axis == 0, along_z, along_x)

    def copy(self, k, f, part, phase, slot, to, src=None):
        s = 0 if self.once else k
        dst = self.at(k, f, part)
        return remote(dst if src is None else src, dst, self.sems[phase].at[s, slot], self.arrive.at[k, f], {"front": to})

    def arrival(self, k, f):
        return pltpu.make_async_copy(self.at(k, f, None), self.at(k, f, None), self.arrive.at[k, f])

    def plan(self, phase):
        x, z = self.x, self.z
        if phase == 0:
            return [(self.me, None, 0, self.near(self.parity, 1)), (self.me, None, 1, self.near(self.parity, 3))]
        if phase == 1:
            r = 1 - self.parity
            return [(self.near(r, 3), 0, 0, self.near(r, 1)), (self.near(r, 1), 1, 1, self.near(r, 3))]
        out = []
        if phase == 2:
            for j in range(2):
                f = x * 4 + x % 2 + 2 * j
                g = ((z + 1) % 2 + 2 * j) * 4 + z
                for d, i in ((1, 0), (3, 1)):
                    out.append((f, None, 4 * j + i, self.near(1, d)))
                for d, i in ((1, 2), (3, 3)):
                    out.append((g, None, 4 * j + i, self.near(0, d)))
            return out
        for j in range(2):
            for d, part in ((3, 0), (1, 1)):
                back = 4 - d
                xs, zs = (x + d) % 4, (z + d) % 4
                out.append((xs * 4 + xs % 2 + 2 * j, part, 4 * j + part, self.near(1, back)))
                out.append((((zs + 1) % 2 + 2 * j) * 4 + zs, part, 4 * j + 2 + part, self.near(0, back)))
        return out

    def start(self, phase, k, src=None):
        seen = None
        for f, part, slot, to in self.plans[phase]:
            new = f is not seen
            seen = f

            @self.when(k, f)
            def _():
                if new and phase in (1, 3):
                    self.arrival(k, f).wait()
                if new and phase == 2:
                    @pl.when(f == self.me)
                    def _():
                        self.own_ready(k)

                    @pl.when((f == self.opposite[0]) | (f == self.opposite[1]))
                    def _():
                        self.arrival(k, f).wait()
                if self.once:
                    @pl.when(k > 0)
                    def _():
                        self.copy(k - 1, f, part, phase, slot, to, src).wait_send()
                self.copy(k, f, part, phase, slot, to, src).start()

    def finish(self, k, lo, hi):
        for f in self.final:
            @pl.when(self.has(k, f) & (f >= lo) & (f < hi) if self.has else True)
            def _():
                self.arrival(k, f).wait()

    def when(self, k, f):
        if self.has:
            return pl.when(self.has(k, f))
        return lambda body: body()

    def prologue(self, first):
        first(0)
        self.start(1, 0)
        first(1)
        self.start(2, 0)
        self.start(1, 1)
        first(2)
        self.start(3, 0)
        self.start(2, 1)
        self.start(1, 2)
        first(3)

    def ahead(self, s, wide, first):
        j = s // 3

        @pl.when(s % 3 == 0)
        def _():
            @pl.when(j + 2 < wide)
            def _():
                self.start(2, j + 2)

            @pl.when(j + 3 < wide)
            def _():
                self.start(1, j + 3)

            @pl.when(j + 4 < wide)
            def _():
                first(j + 4)

        @pl.when((s % 3 == 1) & (j + 1 < wide))
        def _():
            self.start(3, j + 1)

    def drain(self, k, src=None):
        for phase in range(4):
            for f, part, slot, to in self.plans[phase]:
                @self.when(k, f)
                def _():
                    self.copy(k, f, part, phase, slot, to, src if phase == 0 else None).wait_send()


def square_sems(n):
    return [pltpu.SemaphoreType.DMA((n, c)) for c in (2, 2, 8, 8)]


def child_kernel(n, m, land, groups, a_ref, c_ref, hit_ref, l_out, c_out, reach, G, LG, own_sem, arrive, land_arrive, *more):
    sems, land_sems, scratch = more[:4], more[4:8], more[8:]
    T, Lh, Ll = scratch[0], scratch[1], scratch[2]
    stages, rows_own, wide = n // 128, n // groups, n // 256
    me = lax.axis_index("front")
    meet((("front", groups),))

    def part_of(ref, k, f, size, part):
        if part is None:
            return ref.at[k, dynamic(f, size), :]
        return ref.at[k, dynamic(2 * f + part, size // 2), :]

    def own_copy(k):
        return pltpu.make_async_copy(a_ref.at[:, dynamic(k, 256)], G.at[k, dynamic(me, rows_own), :], own_sem.at[k])

    def has(k, f):
        return f // 2 >= k
    rows = Square(lambda k, f, part: part_of(G, k, f, rows_own, part), arrive, sems, has, lambda k: own_copy(k).wait(), False)
    lands = Square(lambda k, f, part: part_of(LG, k, f, land, part), land_arrive, land_sems,
                   None, nothing, True)

    def first(k):
        rows.start(0, k, a_ref.at[:, dynamic(k, 256)])

        @pl.when(has(k, me))
        def _():
            own_copy(k).start()

    def land_use(k):
        lands.finish(k, 0, groups)
        cols = dynamic(k, 256)
        gh, gl = split(LG[k])
        reach[...] = reach[...] - dot3(Lh[n:n + m, cols], Ll[n:n + m, cols], gh, gl)

    def catch_up(p, late, long, short, body):
        def upto(q):
            return jnp.maximum(jnp.where(q >= late, (q - short) // 2, (q - long) // 2) + 1, 0)

        def step(q, _):
            body(q)
            return 0
        lax.fori_loop(upto(p - 1), upto(p), step, 0)

    rows.prologue(first)
    reach[...] = jnp.zeros_like(reach)

    def before(p):
        @pl.when(p % 2 == 0)
        def _():
            rows.finish(p // 2, p, p + 2)

    def after_factor(p):
        rows.ahead(2 * p, wide, first)
        catch_up(p, 12, 3, 2, lambda k: lands.start(1, k))
        catch_up(p, 13, 6, 3, lambda k: lands.start(3, k))

    def before_rest(p):
        @pl.when(p % 2 == 0)
        def _():
            rows.finish(p // 2, p + 2, groups)

    def stage(p, _):
        chol_stage(
            p, n, m,
            lambda kk, rows: G[kk, rows, :],
            lambda kk: c_ref[:, 256 * kk:256 * kk + 256],
            *scratch, before=before, after_factor=after_factor, before_rest=before_rest,
        )
        put_rows(p, n, m, rows_own, me * rows_own, T, l_out, c_out)
        k = p // 2

        @pl.when(p % 2 == 1)
        def _():
            cols = dynamic(k, 256)
            nn = functools.partial(jnp.dot, preferred_element_type=F32)
            LG[k, dynamic(me, land), :] = nn(hit_ref[...], Lh[n:n + m, cols]) + nn(hit_ref[...], Ll[n:n + m, cols])
        rows.ahead(2 * p + 1, wide, first)
        catch_up(p, 12, 4, 2, lambda k: lands.start(2, k))
        catch_up(p, 14, 7, 4, land_use)

        @pl.when(p % 2 == 1)
        def _():
            lands.start(0, k)
        return 0
    lax.fori_loop(0, stages, stage, 0)
    last = wide - 1
    lands.start(1, last)
    land_use(last - 1)
    lands.start(2, last)
    lands.start(3, last)
    land_use(last)
    lands.drain(last)

    def drain(k, _):
        rows.drain(k, a_ref.at[:, dynamic(k, 256)])
        return 0
    lax.fori_loop(0, wide, drain, 0)


def child_call(n, m, land, groups, side):
    dma = pltpu.SemaphoreType.DMA
    vmem = pl.BlockSpec(memory_space=pltpu.VMEM)
    return pl.pallas_call(
        functools.partial(child_kernel, n, m, land, groups),
        out_shape=[jax.ShapeDtypeStruct((n // groups, n), F32), jax.ShapeDtypeStruct((m, n), F32),
                   jax.ShapeDtypeStruct((m, land * groups), F32)],
        in_specs=[pl.BlockSpec(memory_space=pl.ANY), vmem, vmem],
        out_specs=[vmem] * 3,
        scratch_shapes=[
            pltpu.VMEM((n // 256, n, 256), F32), pltpu.VMEM((n // 256, land * groups, 256), F32),
            dma((n // 256,)), dma((n // 256, groups)), dma((n // 256, groups)),
        ] + square_sems(n // 256) + square_sems(1) + chol_scratch(n, m),
        compiler_params=pltpu.CompilerParams(vmem_limit_bytes=62 << 20, collective_id=0, has_side_effects=True),
    )


def parent_kernel(n, m, groups, bulks, reach, route, masked, out, PV, TP, RS, SB, RB, XH, XL, EH, EL,
                  scatter_send, scatter_come, gather_send, gather_come, spread_send, spread_come, arrive, *more):
    sems, scratch = more[:4], more[4:]
    T, Lh, Ll, U, E, ES, LS = scratch
    wide, full = n // 256, n // 128
    me, here = lax.axis_index("front"), lax.axis_index("bulk")
    meet((("front", groups), ("bulk", bulks)))
    nn = functools.partial(jnp.dot, preferred_element_type=F32)
    rh, rl = split(reach[...])

    def slot(b):
        r = route[b * m:(b + 1) * m, :]
        return nn(r, rh) + nn(r, rl)

    def other(d):
        return (here + d) % bulks

    def needed(j):
        return j // 2 <= me // 4

    def scatter(d):
        j = other(d)
        return remote(TP.at[j], RS.at[here], scatter_send.at[d - 1], scatter_come.at[here], {"bulk": j})

    def scattered(b):
        return pltpu.make_async_copy(RS.at[b], RS.at[b], scatter_come.at[b])

    def piece(j):
        return PV.at[j // 2, dynamic(me, m), dynamic(j % 2, 128)]

    def gather(d):
        return remote(piece(here), piece(here), gather_send.at[d - 1], gather_come.at[here], {"bulk": other(d)})

    def spread(d):
        b = other(d)
        return remote(SB.at[b], RB.at[here], spread_send.at[d - 1], spread_come.at[here], {"bulk": b})

    def spreaded(b):
        return pltpu.make_async_copy(RB.at[b], RB.at[b], spread_come.at[b])

    top = slot(0) + jnp.where(here == 0, masked[...], 0.0)
    for j in range(full):
        TP[j] = top[:, 128 * j:128 * j + 128]
    for d in range(1, bulks):
        @pl.when(needed(other(d)))
        def _():
            scatter(d).start()
    for b in range(1, bulks):
        SB[b] = slot(b)

    @pl.when(needed(here))
    def _():
        RS[here] = TP[here]
        for d in range(1, bulks):
            scattered(other(d)).wait()
        total = RS[0]
        for b in range(1, bulks):
            total = total + RS[b]
        PV[here // 2, dynamic(me, m), dynamic(here % 2, 128)] = total
        for d in range(1, bulks):
            gather(d).start()
    for d in range(1, bulks):
        j = other(d)

        @pl.when(needed(j))
        def _():
            pltpu.make_async_copy(piece(j), piece(j), gather_come.at[j]).wait()

    def part_at(k, f, part):
        if part is None:
            return PV.at[k, dynamic(f, m), :]
        return PV.at[k, dynamic(2 * f + part, m // 2), :]
    rows = Square(part_at, arrive, sems, lambda k, f: f // 4 >= k, nothing, False)

    def first(k):
        rows.start(0, k)
    first(0)
    for d in range(1, bulks):
        @pl.when(other(d) != 0)
        def _():
            spread(d).start()
    rows.start(1, 0)
    first(1)
    rows.start(2, 0)
    rows.start(1, 1)
    first(2)
    rows.start(3, 0)
    rows.start(2, 1)
    rows.start(1, 2)
    first(3)

    def before(p):
        @pl.when(p % 2 == 0)
        def _():
            rows.finish(p // 2, 2 * p, 2 * p + 4)

    def before_rest(p):
        @pl.when(p % 2 == 0)
        def _():
            rows.finish(p // 2, 2 * p + 4, groups)

    def stage(p, _):
        chol_stage(p, n, 0, lambda kk, r: PV[kk, r, :], None, *scratch, before=before,
                   after_factor=lambda p: rows.ahead(2 * p, wide, first), before_rest=before_rest)
        EH[p] = ES[0:128, 0:128]
        EL[p] = ES[128:256, 0:128]
        mine = T[dynamic(me, m), dynamic(p % 2, 128)]
        out[:, dynamic(p, 128)] = jnp.where(p * 128 < (me + 1) * m, mine, 0.0)
        rows.ahead(2 * p + 1, wide, first)
        return 0
    lax.fori_loop(0, full, stage, 0)

    @pl.when(here != 0)
    def _():
        for d in range(1, bulks):
            spreaded(other(d)).wait()
        RB[here] = SB[here]
        x = masked[...]
        for b in range(bulks):
            x = x + RB[b]
        for p in range(full):
            cols = slice(128 * p, 128 * p + 128)
            y = x[:, cols]
            if p:
                y = y - dot3(XH[:, :128 * p], XL[:, :128 * p], Lh[cols, :128 * p], Ll[cols, :128 * p])
            yh, yl = split(y)
            y = dot3(yh, yl, EH[p], EL[p])
            out[:, cols] = y
            yh, yl = split(y)
            XH[:, cols] = yh
            XL[:, cols] = yl
    for d in range(1, bulks):
        @pl.when(needed(other(d)))
        def _():
            scatter(d).wait_send()

        @pl.when(needed(here))
        def _():
            gather(d).wait_send()

        @pl.when(other(d) != 0)
        def _():
            spread(d).wait_send()

    def drain(k, _):
        rows.drain(k)
        return 0
    lax.fori_loop(0, wide, drain, 0)


def parent_call(n, m, groups, bulks):
    dma = pltpu.SemaphoreType.DMA
    vmem = pl.BlockSpec(memory_space=pltpu.VMEM)
    full, wide = n // 128, n // 256
    return pl.pallas_call(
        functools.partial(parent_kernel, n, m, groups, bulks),
        out_shape=jax.ShapeDtypeStruct((m, n), F32),
        in_specs=[vmem] * 3,
        out_specs=vmem,
        scratch_shapes=[
            pltpu.VMEM((wide, n, 256), F32), pltpu.VMEM((full, m, 128), F32), pltpu.VMEM((bulks, m, 128), F32),
            pltpu.VMEM((bulks, m, n), F32), pltpu.VMEM((bulks, m, n), F32), pltpu.VMEM((m, n), BF), pltpu.VMEM((m, n), BF),
            pltpu.VMEM((full, 128, 128), BF), pltpu.VMEM((full, 128, 128), BF),
            dma((bulks - 1,)), dma((bulks,)), dma((bulks - 1,)), dma((bulks,)), dma((bulks - 1,)), dma((bulks,)),
            dma((wide, groups)),
        ] + square_sems(wide) + chol_scratch(n, 0),
        compiler_params=pltpu.CompilerParams(vmem_limit_bytes=40 << 20, collective_id=1, has_side_effects=True),
    )


def on_device(child_pivot, child_coupling, parent_arrow, row_map, block_pattern):
    own_rows = child_pivot[0]
    parent_index = row_map[0]
    row_count, pivot_count = own_rows.shape
    parent_count, pivots = parent_arrow.shape
    front_index = lax.axis_index("front")
    front_groups = lax.axis_size("front")
    slot_index = (
        parent_index // parent_count // front_groups * parent_count + parent_index % parent_count
    )
    spread_rows = lax.axis_size("bulk") * parent_count
    routing = (jnp.arange(spread_rows)[:, None] == slot_index[None, :]).astype(BF)
    lower_rows, coupling, reached = child_call(pivot_count, row_count, parent_count, front_groups, 4)(
        own_rows, child_coupling[0], routing[:parent_count]
    )
    device_index = lax.axis_index("bulk") * front_groups + front_index
    first_row = device_index * parent_count
    block_rows = (first_row + jnp.arange(parent_count)) // BLOCK
    picker = (block_rows[:, None] == jnp.arange(block_pattern.shape[0])[None, :]).astype(F32)
    row_mask = jnp.dot(picker, block_pattern.astype(F32), precision=HIGHEST_PRECISION)
    masked = parent_arrow * jnp.repeat(row_mask, BLOCK, axis=1)
    parent_rows = parent_call(pivots, parent_count, front_groups, lax.axis_size("bulk"))(reached, routing, masked)
    return (lower_rows[None], coupling[None], parent_rows)


def solution(mesh):
    placed = (
        P("bulk", "front", None),
        P("bulk", "front", None),
        P(("bulk", "front"), None),
        P("bulk", "front"),
        P(),
    )
    return jax.shard_map(
        on_device,
        mesh=mesh,
        in_specs=placed,
        out_specs=(P("bulk", "front", None), P("bulk", "front", None), P(("bulk", "front"), None)),
        check_vma=False,
    )
```

```python
import functools

import jax
import jax.numpy as jnp
from jax import lax
from jax.experimental import pallas as pl
from jax.experimental.pallas import tpu as pltpu
from jax.sharding import PartitionSpec as P

BLOCK = 128
F32, BF = jnp.float32, jnp.bfloat16
NT = (((1,), (1,)), ((), ()))
MESH = pl.DeviceIdType.MESH
HIGHEST_PRECISION = lax.Precision.HIGHEST


def factor_block(load_row, store_u, store_e, n=128, sb=8):
    nb = n // sb
    W = [load_row(v) for v in range(nb)]
    lane = lax.broadcasted_iota(jnp.int32, (sb, n), 1)
    sub = lax.broadcasted_iota(jnp.int32, (sb, n), 0)
    for b in range(nb):
        base = b * sb
        inblk = (lane >= base) & (lane < base + sb)
        R = W[b]
        S = [jnp.broadcast_to(R[:, base + j:base + j + 1], (sb, n)) for j in range(sb)]
        F = {}
        for j in range(sb):
            for i in range(j, sb):
                F[i, j] = jnp.broadcast_to(S[j][i:i + 1, :], (sb, n))
        rinv = []
        for j in range(sb):
            r = lax.rsqrt(F[j, j])
            rinv.append(r)
            for i in range(j, sb):
                F[i, j] = F[i, j] * r
            for c in range(j + 1, sb):
                for i in range(c, sb):
                    F[i, c] = F[i, c] - F[i, j] * F[c, j]
        RI = jnp.where(inblk, (lane - base == sub).astype(jnp.float32), R)
        u = []
        for j in range(sb):
            t = jnp.broadcast_to(RI[j:j + 1, :], (sb, n))
            for m in range(j):
                t = t - F[j, m] * u[m]
            u.append(t * rinv[j])
        e = u[0]
        for j in range(1, sb):
            e = jnp.where(sub == j, u[j], e)
        store_e(b, jnp.where(lane < base + sb, e, 0.0))
        d = jnp.zeros((sb, n), jnp.float32)
        for c in range(sb):
            col = F[c, 0]
            for j in range(1, c + 1):
                col = jnp.where(sub == j, F[c, j], col)
            d = jnp.where((lane == base + c) & (sub <= c), col, d)
        store_u(b, jnp.where(inblk, d, jnp.where(lane < base, 0.0, e)))
        for v in range(b + 1, nb):
            C = []
            acc = jnp.where(inblk, 0.0, W[v])
            for j in range(sb):
                c = jnp.broadcast_to(W[v][:, base + j:base + j + 1], (sb, n))
                for m in range(j):
                    c = c - C[m] * F[j, m]
                c = c * rinv[j]
                C.append(c)
                acc = acc - c * u[j]
            W[v] = acc


def split(x):
    hi = x.astype(BF)
    return hi, (x - hi.astype(F32)).astype(BF)

def dot3(ah, al, bh, bl):
    d = functools.partial(lax.dot_general, dimension_numbers=NT, preferred_element_type=F32)
    return d(ah, bh) + (d(ah, bl) + d(al, bh))


def dynamic(p, size):
    return pl.ds(pl.multiple_of(p * size, size), size)


def stack(ref, bh, bl):
    ref[0:128, 0:128] = bh
    ref[0:128, 128:256] = bh
    ref[128:256, 0:128] = bl
    ref[128:256, 128:256] = jnp.zeros_like(bl)


def dot_stacked(ah, al, ref):
    y = lax.dot_general(jnp.concatenate([ah, al], axis=1), ref[...], NT, preferred_element_type=F32)
    return y[:, :128] + y[:, 128:]


def chol_stage(p, n, m, block, extra, T, Lh, Ll, U, E, ES, LS, *, before, after_factor, before_rest):
    full = n // 256
    k, half = p // 2, p % 2
    prow = pl.multiple_of(p * 128, 128)
    pcol = pl.ds(prow, 128)
    qcol = pl.ds(pl.multiple_of(prow - half * 128, 128), 128)
    hcol = dynamic(half, 128)

    def update(kk, r, cnt):
        rows = pl.ds(r, cnt)
        x = extra(kk) if isinstance(r, int) and r >= n else block(kk, rows)
        if kk:
            kr = pl.ds(256 * kk, 256)
            x = x - dot3(Lh[rows, :256 * kk], Ll[rows, :256 * kk], Lh[kr, :256 * kk], Ll[kr, :256 * kk])
        T[rows, :] = x

    def half_update(r, cnt):
        rows = pl.ds(r, cnt)
        T[rows, 128:256] = T[rows, 128:256] - dot_stacked(Lh[rows, qcol], Ll[rows, qcol], LS)

    def solve(r, cnt):
        rows = pl.ds(r, cnt)
        th, tl = split(T[rows, hcol])
        x = dot_stacked(th, tl, ES)
        T[rows, hcol] = x
        xh, xl = split(x)
        Lh[rows, pcol] = xh
        Ll[rows, pcol] = xl

    def rest(first, body):
        count = full - first

        def step(i, _):
            body(pl.multiple_of(first * 256 + i * 512, 256), 512)
            return 0
        lax.fori_loop(0, count // 2, step, 0)
        if not isinstance(first, int):
            pl.when(count % 2 == 1)(lambda: body(n - 256, 256))
        elif count % 2:
            body(n - 256, 256)
        if m:
            body(n, m)

    before(p)
    for kk in range(full):
        @pl.when(p == 2 * kk)
        def _():
            update(kk, 256 * kk, 256)

    @pl.when(half == 1)
    def _():
        stack(LS, Lh[pcol, qcol], Ll[pcol, qcol])
        half_update(prow, 128)

    def su(b, x): U[pl.ds(8 * b, 8), :] = x
    def se(b, x): E[pl.ds(8 * b, 8), :] = x
    factor_block(lambda v: T[pl.ds(pl.multiple_of(prow + 8 * v, 8), 8), hcol], su, se)
    stack(ES, *split(E[...]))
    after_factor(p)

    @pl.when(half == 0)
    def _():
        solve(pl.multiple_of(prow + 128, 128), 128)
    before_rest(p)
    for kk in range(full):
        @pl.when(p == 2 * kk)
        def _():
            def both(r, cnt):
                update(kk, r, cnt)
                solve(r, cnt)
            rest(kk + 1, both)

    @pl.when(half == 1)
    def _():
        def both(r, cnt):
            half_update(r, cnt)
            solve(r, cnt)
        rest(k + 1, both)
    T[pl.ds(prow, 128), hcol] = U[...].T


def put_rows(p, n, m, own, row0, T, l_out, c_out):
    hcol, pcol = dynamic(p % 2, 128), dynamic(p, 128)
    c_out[:, pcol] = T[n:n + m, hcol]
    mine = T[pl.ds(pl.multiple_of(row0, own), own), hcol]
    l_out[:, pcol] = jnp.where(p * 128 < row0 + own, mine, 0.0)


def chol_scratch(n, m):
    return [pltpu.VMEM((n + m, 256), F32), pltpu.VMEM((n + m, n), BF), pltpu.VMEM((n + m, n), BF),
            pltpu.VMEM((128, 128), F32), pltpu.VMEM((128, 128), F32),
            pltpu.VMEM((256, 256), BF), pltpu.VMEM((256, 256), BF)]


def nothing(p):
    pass


def remote(src, dst, send_sem, recv_sem, to):
    return pltpu.make_async_remote_copy(src_ref=src, dst_ref=dst, send_sem=send_sem, recv_sem=recv_sem,
                                        device_id=to, device_id_type=MESH)


def meet(axes):
    barrier = pltpu.get_barrier_semaphore()
    count = 0
    for axis, size in axes:
        here = lax.axis_index(axis)
        for d in range(1, size):
            pl.semaphore_signal(barrier, inc=1, device_id={axis: (here + d) % size}, device_id_type=MESH)
        count += size - 1
    pl.semaphore_wait(barrier, count)


class Square:
    def __init__(self, at, arrive, sems, has, own_ready, once):
        self.at, self.arrive, self.sems, self.has, self.own_ready, self.once = at, arrive, sems, has, own_ready, once
        me = lax.axis_index("front")
        self.me, self.x, self.z = me, me // 4, me % 4
        self.parity = (self.x + self.z) % 2
        self.plans = [self.plan(phase) for phase in range(4)]
        self.opposite = self.near(0, 2), self.near(1, 2)
        xs, zs = (self.x + 2) % 4, (self.z + 2) % 4
        self.final = [f for j in range(2) for f in (xs * 4 + xs % 2 + 2 * j, ((zs + 1) % 2 + 2 * j) * 4 + zs)]

    def near(self, axis, d):
        along_z = self.x * 4 + (self.z + d) % 4
        along_x = (self.x + d) % 4 * 4 + self.z
        if isinstance(axis, int):
            return along_x if axis else along_z
        return jnp.where(axis == 0, along_z, along_x)

    def copy(self, k, f, part, phase, slot, to, src=None):
        s = 0 if self.once else k
        dst = self.at(k, f, part)
        return remote(dst if src is None else src, dst, self.sems[phase].at[s, slot], self.arrive.at[k, f], {"front": to})

    def arrival(self, k, f):
        return pltpu.make_async_copy(self.at(k, f, None), self.at(k, f, None), self.arrive.at[k, f])

    def plan(self, phase):
        x, z = self.x, self.z
        if phase == 0:
            return [(self.me, None, 0, self.near(self.parity, 1)), (self.me, None, 1, self.near(self.parity, 3))]
        if phase == 1:
            r = 1 - self.parity
            return [(self.near(r, 3), 0, 0, self.near(r, 1)), (self.near(r, 1), 1, 1, self.near(r, 3))]
        out = []
        if phase == 2:
            for j in range(2):
                f = x * 4 + x % 2 + 2 * j
                g = ((z + 1) % 2 + 2 * j) * 4 + z
                for d, i in ((1, 0), (3, 1)):
                    out.append((f, None, 4 * j + i, self.near(1, d)))
                for d, i in ((1, 2), (3, 3)):
                    out.append((g, None, 4 * j + i, self.near(0, d)))
            return out
        for j in range(2):
            for d, part in ((3, 0), (1, 1)):
                back = 4 - d
                xs, zs = (x + d) % 4, (z + d) % 4
                out.append((xs * 4 + xs % 2 + 2 * j, part, 4 * j + part, self.near(1, back)))
                out.append((((zs + 1) % 2 + 2 * j) * 4 + zs, part, 4 * j + 2 + part, self.near(0, back)))
        return out

    def start(self, phase, k, src=None):
        seen = None
        for f, part, slot, to in self.plans[phase]:
            new = f is not seen
            seen = f

            @self.when(k, f)
            def _():
                if new and phase in (1, 3):
                    self.arrival(k, f).wait()
                if new and phase == 2:
                    @pl.when(f == self.me)
                    def _():
                        self.own_ready(k)

                    @pl.when((f == self.opposite[0]) | (f == self.opposite[1]))
                    def _():
                        self.arrival(k, f).wait()
                if self.once:
                    @pl.when(k > 0)
                    def _():
                        self.copy(k - 1, f, part, phase, slot, to, src).wait_send()
                self.copy(k, f, part, phase, slot, to, src).start()

    def finish(self, k, lo, hi):
        for f in self.final:
            @pl.when(self.has(k, f) & (f >= lo) & (f < hi) if self.has else True)
            def _():
                self.arrival(k, f).wait()

    def when(self, k, f):
        if self.has:
            return pl.when(self.has(k, f))
        return lambda body: body()

    def prologue(self, first):
        first(0)
        first(1)
        self.start(1, 0)
        self.start(2, 0)
        self.start(1, 1)
        first(2)
        self.start(3, 0)
        self.start(2, 1)
        self.start(1, 2)
        first(3)

    def ahead(self, s, wide, first):
        j = s // 3

        @pl.when(s % 3 == 0)
        def _():
            @pl.when(j + 2 < wide)
            def _():
                self.start(2, j + 2)

            @pl.when(j + 3 < wide)
            def _():
                self.start(1, j + 3)

            @pl.when(j + 4 < wide)
            def _():
                first(j + 4)

        @pl.when((s % 3 == 2) & (j + 1 < wide))
        def _():
            self.start(3, j + 1)

    def drain(self, k, src=None):
        for phase in range(4):
            for f, part, slot, to in self.plans[phase]:
                @self.when(k, f)
                def _():
                    self.copy(k, f, part, phase, slot, to, src if phase == 0 else None).wait_send()


def square_sems(n):
    return [pltpu.SemaphoreType.DMA((n, c)) for c in (2, 2, 8, 8)]


def child_kernel(n, m, land, groups, a_ref, c_ref, hit_ref, l_out, c_out, reach, G, LG, own_sem, arrive, land_arrive, *more):
    sems, land_sems, scratch = more[:4], more[4:8], more[8:]
    T, Lh, Ll = scratch[0], scratch[1], scratch[2]
    stages, rows_own, wide = n // 128, n // groups, n // 256
    me = lax.axis_index("front")
    meet((("front", groups),))

    def part_of(ref, k, f, size, part):
        if part is None:
            return ref.at[k, dynamic(f, size), :]
        return ref.at[k, dynamic(2 * f + part, size // 2), :]

    def own_copy(k):
        return pltpu.make_async_copy(a_ref.at[:, dynamic(k, 256)], G.at[k, dynamic(me, rows_own), :], own_sem.at[k])

    def has(k, f):
        return f // 2 >= k
    rows = Square(lambda k, f, part: part_of(G, k, f, rows_own, part), arrive, sems, has, lambda k: own_copy(k).wait(), False)
    lands = Square(lambda k, f, part: part_of(LG, k, f, land, part), land_arrive, land_sems,
                   None, nothing, True)

    def first(k):
        rows.start(0, k, a_ref.at[:, dynamic(k, 256)])

        @pl.when(has(k, me))
        def _():
            own_copy(k).start()

    def land_use(k):
        lands.finish(k, 0, groups)
        cols = dynamic(k, 256)
        gh, gl = split(LG[k])
        reach[...] = reach[...] - dot3(Lh[n:n + m, cols], Ll[n:n + m, cols], gh, gl)

    def catch_up(p, late, long, short, body):
        def upto(q):
            return jnp.maximum(jnp.where(q >= late, (q - short) // 2, (q - long) // 2) + 1, 0)

        def step(q, _):
            body(q)
            return 0
        lax.fori_loop(upto(p - 1), upto(p), step, 0)

    rows.prologue(first)
    reach[...] = jnp.zeros_like(reach)

    def before(p):
        @pl.when(p % 2 == 0)
        def _():
            rows.finish(p // 2, p, p + 2)

    def after_factor(p):
        rows.ahead(2 * p, wide, first)
        catch_up(p, 12, 3, 2, lambda k: lands.start(1, k))
        catch_up(p, 13, 6, 3, lambda k: lands.start(3, k))

    def before_rest(p):
        @pl.when(p % 2 == 0)
        def _():
            rows.finish(p // 2, p + 2, groups)

    def stage(p, _):
        chol_stage(
            p, n, m,
            lambda kk, rows: G[kk, rows, :],
            lambda kk: c_ref[:, 256 * kk:256 * kk + 256],
            *scratch, before=before, after_factor=after_factor, before_rest=before_rest,
        )
        put_rows(p, n, m, rows_own, me * rows_own, T, l_out, c_out)
        k = p // 2

        @pl.when(p % 2 == 1)
        def _():
            cols = dynamic(k, 256)
            nn = functools.partial(jnp.dot, preferred_element_type=F32)
            hits = hit_ref[0:land, :]
            LG[k, dynamic(me, land), :] = nn(hits, Lh[n:n + m, cols]) + nn(hits, Ll[n:n + m, cols])
        rows.ahead(2 * p + 1, wide, first)
        catch_up(p, 12, 4, 2, lambda k: lands.start(2, k))
        catch_up(p, 14, 7, 4, land_use)

        @pl.when(p % 2 == 1)
        def _():
            lands.start(0, k)
        return 0
    lax.fori_loop(0, stages, stage, 0)
    last = wide - 1
    lands.start(1, last)
    land_use(last - 1)
    lands.start(2, last)
    lands.start(3, last)
    land_use(last)
    lands.drain(last)

    def drain(k, _):
        rows.drain(k, a_ref.at[:, dynamic(k, 256)])
        return 0
    lax.fori_loop(0, wide, drain, 0)


def child_call(n, m, land, groups, side):
    dma = pltpu.SemaphoreType.DMA
    vmem = pl.BlockSpec(memory_space=pltpu.VMEM)
    return pl.pallas_call(
        functools.partial(child_kernel, n, m, land, groups),
        out_shape=[jax.ShapeDtypeStruct((n // groups, n), F32), jax.ShapeDtypeStruct((m, n), F32),
                   jax.ShapeDtypeStruct((m, land * groups), F32)],
        in_specs=[pl.BlockSpec(memory_space=pl.ANY), vmem, vmem],
        out_specs=[vmem] * 3,
        scratch_shapes=[
            pltpu.VMEM((n // 256, n, 256), F32), pltpu.VMEM((n // 256, land * groups, 256), F32),
            dma((n // 256,)), dma((n // 256, groups)), dma((n // 256, groups)),
        ] + square_sems(n // 256) + square_sems(1) + chol_scratch(n, m),
        compiler_params=pltpu.CompilerParams(vmem_limit_bytes=62 << 20, collective_id=0, has_side_effects=True),
    )


def parent_kernel(n, m, groups, bulks, reach, route, masked, out, PV, TP, RS, SB, RB, XH, XL, EH, EL,
                  scatter_send, scatter_come, gather_send, gather_come, spread_send, spread_come, arrive, *more):
    sems, scratch = more[:4], more[4:]
    T, Lh, Ll, U, E, ES, LS = scratch
    wide, full = n // 256, n // 128
    me, here = lax.axis_index("front"), lax.axis_index("bulk")
    meet((("front", groups), ("bulk", bulks)))
    nn = functools.partial(jnp.dot, preferred_element_type=F32)
    rh, rl = split(reach[...])

    def slot(b):
        r = route[b * m:(b + 1) * m, :]
        return nn(r, rh) + nn(r, rl)

    def other(d):
        return (here + d) % bulks

    def needed(j):
        return j // 2 <= me // 4

    def scatter(d):
        j = other(d)
        return remote(TP.at[j], RS.at[here], scatter_send.at[d - 1], scatter_come.at[here], {"bulk": j})

    def scattered(b):
        return pltpu.make_async_copy(RS.at[b], RS.at[b], scatter_come.at[b])

    def piece(j):
        return PV.at[j // 2, dynamic(me, m), dynamic(j % 2, 128)]

    def gather(d):
        return remote(piece(here), piece(here), gather_send.at[d - 1], gather_come.at[here], {"bulk": other(d)})

    def spread(d):
        b = other(d)
        return remote(SB.at[b], RB.at[here], spread_send.at[d - 1], spread_come.at[here], {"bulk": b})

    def spreaded(b):
        return pltpu.make_async_copy(RB.at[b], RB.at[b], spread_come.at[b])

    top = slot(0) + jnp.where(here == 0, masked[...], 0.0)
    for j in range(full):
        TP[j] = top[:, 128 * j:128 * j + 128]
    for d in range(1, bulks):
        @pl.when(needed(other(d)))
        def _():
            scatter(d).start()
    for b in range(1, bulks):
        SB[b] = slot(b)

    @pl.when(needed(here))
    def _():
        RS[here] = TP[here]
        for d in range(1, bulks):
            scattered(other(d)).wait()
        total = RS[0]
        for b in range(1, bulks):
            total = total + RS[b]
        PV[here // 2, dynamic(me, m), dynamic(here % 2, 128)] = total
        for d in range(1, bulks):
            gather(d).start()
    for d in range(1, bulks):
        j = other(d)

        @pl.when(needed(j))
        def _():
            pltpu.make_async_copy(piece(j), piece(j), gather_come.at[j]).wait()

    def part_at(k, f, part):
        if part is None:
            return PV.at[k, dynamic(f, m), :]
        return PV.at[k, dynamic(2 * f + part, m // 2), :]
    rows = Square(part_at, arrive, sems, lambda k, f: f // 4 >= k, nothing, False)

    def first(k):
        rows.start(0, k)
    first(0)
    for d in range(1, bulks):
        @pl.when(other(d) != 0)
        def _():
            spread(d).start()
    rows.start(1, 0)
    first(1)
    rows.start(2, 0)
    rows.start(1, 1)
    first(2)
    rows.start(3, 0)
    rows.start(2, 1)
    rows.start(1, 2)
    first(3)

    def before(p):
        @pl.when(p % 2 == 0)
        def _():
            rows.finish(p // 2, 2 * p, 2 * p + 4)

    def before_rest(p):
        @pl.when(p % 2 == 0)
        def _():
            rows.finish(p // 2, 2 * p + 4, groups)

    def stage(p, _):
        chol_stage(p, n, 0, lambda kk, r: PV[kk, r, :], None, *scratch, before=before,
                   after_factor=lambda p: rows.ahead(2 * p, wide, first), before_rest=before_rest)
        EH[p] = ES[0:128, 0:128]
        EL[p] = ES[128:256, 0:128]
        mine = T[dynamic(me, m), dynamic(p % 2, 128)]
        out[:, dynamic(p, 128)] = jnp.where(p * 128 < (me + 1) * m, mine, 0.0)
        rows.ahead(2 * p + 1, wide, first)
        return 0
    lax.fori_loop(0, full, stage, 0)

    @pl.when(here != 0)
    def _():
        for d in range(1, bulks):
            spreaded(other(d)).wait()
        RB[here] = SB[here]
        x = masked[...]
        for b in range(bulks):
            x = x + RB[b]
        for p in range(full):
            cols = slice(128 * p, 128 * p + 128)
            y = x[:, cols]
            if p:
                y = y - dot3(XH[:, :128 * p], XL[:, :128 * p], Lh[cols, :128 * p], Ll[cols, :128 * p])
            yh, yl = split(y)
            y = dot3(yh, yl, EH[p], EL[p])
            out[:, cols] = y
            yh, yl = split(y)
            XH[:, cols] = yh
            XL[:, cols] = yl
    for d in range(1, bulks):
        @pl.when(needed(other(d)))
        def _():
            scatter(d).wait_send()

        @pl.when(needed(here))
        def _():
            gather(d).wait_send()

        @pl.when(other(d) != 0)
        def _():
            spread(d).wait_send()

    def drain(k, _):
        rows.drain(k)
        return 0
    lax.fori_loop(0, wide, drain, 0)


def parent_call(n, m, groups, bulks):
    dma = pltpu.SemaphoreType.DMA
    vmem = pl.BlockSpec(memory_space=pltpu.VMEM)
    full, wide = n // 128, n // 256
    return pl.pallas_call(
        functools.partial(parent_kernel, n, m, groups, bulks),
        out_shape=jax.ShapeDtypeStruct((m, n), F32),
        in_specs=[vmem] * 3,
        out_specs=vmem,
        scratch_shapes=[
            pltpu.VMEM((wide, n, 256), F32), pltpu.VMEM((full, m, 128), F32), pltpu.VMEM((bulks, m, 128), F32),
            pltpu.VMEM((bulks, m, n), F32), pltpu.VMEM((bulks, m, n), F32), pltpu.VMEM((m, n), BF), pltpu.VMEM((m, n), BF),
            pltpu.VMEM((full, 128, 128), BF), pltpu.VMEM((full, 128, 128), BF),
            dma((bulks - 1,)), dma((bulks,)), dma((bulks - 1,)), dma((bulks,)), dma((bulks - 1,)), dma((bulks,)),
            dma((wide, groups)),
        ] + square_sems(wide) + chol_scratch(n, 0),
        compiler_params=pltpu.CompilerParams(vmem_limit_bytes=40 << 20, collective_id=1, has_side_effects=True),
    )


def on_device(child_pivot, child_coupling, parent_arrow, row_map, block_pattern):
    own_rows = child_pivot[0]
    parent_index = row_map[0]
    row_count, pivot_count = own_rows.shape
    parent_count, pivots = parent_arrow.shape
    front_index = lax.axis_index("front")
    front_groups = lax.axis_size("front")
    slot_index = (
        parent_index // parent_count // front_groups * parent_count + parent_index % parent_count
    )
    spread_rows = lax.axis_size("bulk") * parent_count
    routing = (jnp.arange(spread_rows)[:, None] == slot_index[None, :]).astype(BF)
    lower_rows, coupling, reached = child_call(pivot_count, row_count, parent_count, front_groups, 4)(
        own_rows, child_coupling[0], routing
    )
    device_index = lax.axis_index("bulk") * front_groups + front_index
    first_row = device_index * parent_count
    block_rows = (first_row + jnp.arange(parent_count)) // BLOCK
    picker = (block_rows[:, None] == jnp.arange(block_pattern.shape[0])[None, :]).astype(F32)
    row_mask = jnp.dot(picker, block_pattern.astype(F32), precision=HIGHEST_PRECISION)
    masked = parent_arrow * jnp.repeat(row_mask, BLOCK, axis=1)
    parent_rows = parent_call(pivots, parent_count, front_groups, lax.axis_size("bulk"))(reached, routing, masked)
    return (lower_rows[None], coupling[None], parent_rows)


def solution(mesh):
    placed = (
        P("bulk", "front", None),
        P("bulk", "front", None),
        P(("bulk", "front"), None),
        P("bulk", "front"),
        P(),
    )
    return jax.shard_map(
        on_device,
        mesh=mesh,
        in_specs=placed,
        out_specs=(P("bulk", "front", None), P("bulk", "front", None), P(("bulk", "front"), None)),
        check_vma=False,
    )
```

```python
import functools

import jax
import jax.numpy as jnp
from jax import lax
from jax.experimental import pallas as pl
from jax.experimental.pallas import tpu as pltpu
from jax.sharding import PartitionSpec as P

BLOCK = 128
F32, BF = jnp.float32, jnp.bfloat16
NT = (((1,), (1,)), ((), ()))
MESH = pl.DeviceIdType.MESH
HIGHEST_PRECISION = lax.Precision.HIGHEST


def factor_block(load_row, store_u, store_e, n=128, sb=8):
    nb = n // sb
    W = [load_row(v) for v in range(nb)]
    lane = lax.broadcasted_iota(jnp.int32, (sb, n), 1)
    sub = lax.broadcasted_iota(jnp.int32, (sb, n), 0)
    for b in range(nb):
        base = b * sb
        inblk = (lane >= base) & (lane < base + sb)
        R = W[b]
        S = [jnp.broadcast_to(R[:, base + j:base + j + 1], (sb, n)) for j in range(sb)]
        F = {}
        for j in range(sb):
            for i in range(j, sb):
                F[i, j] = jnp.broadcast_to(S[j][i:i + 1, :], (sb, n))
        rinv = []
        for j in range(sb):
            r = lax.rsqrt(F[j, j])
            rinv.append(r)
            for i in range(j, sb):
                F[i, j] = F[i, j] * r
            for c in range(j + 1, sb):
                for i in range(c, sb):
                    F[i, c] = F[i, c] - F[i, j] * F[c, j]
        RI = jnp.where(inblk, (lane - base == sub).astype(jnp.float32), R)
        u = []
        for j in range(sb):
            t = jnp.broadcast_to(RI[j:j + 1, :], (sb, n))
            for m in range(j):
                t = t - F[j, m] * u[m]
            u.append(t * rinv[j])
        e = u[0]
        for j in range(1, sb):
            e = jnp.where(sub == j, u[j], e)
        store_e(b, jnp.where(lane < base + sb, e, 0.0))
        d = jnp.zeros((sb, n), jnp.float32)
        for j in range(sb):
            for c in range(j, sb):
                d = jnp.where((sub == j) & (lane == base + c), F[c, j], d)
        store_u(b, jnp.where(inblk, d, jnp.where(lane < base, 0.0, e)))
        for v in range(b + 1, nb):
            C = []
            acc = jnp.where(inblk, 0.0, W[v])
            for j in range(sb):
                c = jnp.broadcast_to(W[v][:, base + j:base + j + 1], (sb, n))
                for m in range(j):
                    c = c - C[m] * F[j, m]
                c = c * rinv[j]
                C.append(c)
                acc = acc - c * u[j]
            W[v] = acc


def split(x):
    hi = x.astype(BF)
    return hi, (x - hi.astype(F32)).astype(BF)

def dot3(ah, al, bh, bl):
    d = functools.partial(lax.dot_general, dimension_numbers=NT, preferred_element_type=F32)
    return d(ah, bh) + (d(ah, bl) + d(al, bh))


def dynamic(p, size):
    return pl.ds(pl.multiple_of(p * size, size), size)


def stack(ref, bh, bl):
    ref[0:128, 0:128] = bh
    ref[0:128, 128:256] = bh
    ref[128:256, 0:128] = bl
    ref[128:256, 128:256] = jnp.zeros_like(bl)


def dot_stacked(ah, al, ref):
    y = lax.dot_general(jnp.concatenate([ah, al], axis=1), ref[...], NT, preferred_element_type=F32)
    return y[:, :128] + y[:, 128:]


def chol_stage(p, n, m, block, extra, T, Lh, Ll, U, E, ES, LS, *, before, after_factor, before_rest):
    full = n // 256
    k, half = p // 2, p % 2
    prow = pl.multiple_of(p * 128, 128)
    pcol = pl.ds(prow, 128)
    qcol = pl.ds(pl.multiple_of(prow - half * 128, 128), 128)
    hcol = dynamic(half, 128)

    def update(kk, r, cnt):
        rows = pl.ds(r, cnt)
        x = extra(kk) if isinstance(r, int) and r >= n else block(kk, rows)
        if kk:
            kr = pl.ds(256 * kk, 256)
            x = x - dot3(Lh[rows, :256 * kk], Ll[rows, :256 * kk], Lh[kr, :256 * kk], Ll[kr, :256 * kk])
        T[rows, :] = x

    def half_update(r, cnt):
        rows = pl.ds(r, cnt)
        T[rows, 128:256] = T[rows, 128:256] - dot_stacked(Lh[rows, qcol], Ll[rows, qcol], LS)

    def solve(r, cnt):
        rows = pl.ds(r, cnt)
        th, tl = split(T[rows, hcol])
        x = dot_stacked(th, tl, ES)
        T[rows, hcol] = x
        xh, xl = split(x)
        Lh[rows, pcol] = xh
        Ll[rows, pcol] = xl

    def rest(first, body):
        count = full - first

        def step(i, _):
            body(pl.multiple_of(first * 256 + i * 512, 256), 512)
            return 0
        lax.fori_loop(0, count // 2, step, 0)
        if not isinstance(first, int):
            pl.when(count % 2 == 1)(lambda: body(n - 256, 256))
        elif count % 2:
            body(n - 256, 256)
        if m:
            body(n, m)

    before(p)
    for kk in range(full):
        @pl.when(p == 2 * kk)
        def _():
            update(kk, 256 * kk, 256)

    @pl.when(half == 1)
    def _():
        stack(LS, Lh[pcol, qcol], Ll[pcol, qcol])
        half_update(prow, 128)

    def su(b, x): U[pl.ds(8 * b, 8), :] = x
    def se(b, x): E[pl.ds(8 * b, 8), :] = x
    factor_block(lambda v: T[pl.ds(pl.multiple_of(prow + 8 * v, 8), 8), hcol], su, se)
    stack(ES, *split(E[...]))
    after_factor(p)

    @pl.when(half == 0)
    def _():
        solve(pl.multiple_of(prow + 128, 128), 128)
    before_rest(p)
    for kk in range(full):
        @pl.when(p == 2 * kk)
        def _():
            def both(r, cnt):
                update(kk, r, cnt)
                solve(r, cnt)
            rest(kk + 1, both)

    @pl.when(half == 1)
    def _():
        def both(r, cnt):
            half_update(r, cnt)
            solve(r, cnt)
        rest(k + 1, both)
    T[pl.ds(prow, 128), hcol] = U[...].T


def put_rows(p, n, m, own, row0, T, l_out, c_out):
    hcol, pcol = dynamic(p % 2, 128), dynamic(p, 128)
    c_out[:, pcol] = T[n:n + m, hcol]
    mine = T[pl.ds(pl.multiple_of(row0, own), own), hcol]
    l_out[:, pcol] = jnp.where(p * 128 < row0 + own, mine, 0.0)


def chol_scratch(n, m):
    return [pltpu.VMEM((n + m, 256), F32), pltpu.VMEM((n + m, n), BF), pltpu.VMEM((n + m, n), BF),
            pltpu.VMEM((128, 128), F32), pltpu.VMEM((128, 128), F32),
            pltpu.VMEM((256, 256), BF), pltpu.VMEM((256, 256), BF)]


def nothing(p):
    pass


def remote(src, dst, send_sem, recv_sem, to):
    return pltpu.make_async_remote_copy(src_ref=src, dst_ref=dst, send_sem=send_sem, recv_sem=recv_sem,
                                        device_id=to, device_id_type=MESH)


def meet(axes):
    barrier = pltpu.get_barrier_semaphore()
    count = 0
    for axis, size in axes:
        here = lax.axis_index(axis)
        for d in range(1, size):
            pl.semaphore_signal(barrier, inc=1, device_id={axis: (here + d) % size}, device_id_type=MESH)
        count += size - 1
    pl.semaphore_wait(barrier, count)


class Square:
    def __init__(self, at, arrive, sems, has, own_ready, once):
        self.at, self.arrive, self.sems, self.has, self.own_ready, self.once = at, arrive, sems, has, own_ready, once
        me = lax.axis_index("front")
        self.me, self.x, self.z = me, me // 4, me % 4
        self.parity = (self.x + self.z) % 2
        self.plans = [self.plan(phase) for phase in range(4)]
        self.opposite = self.near(0, 2), self.near(1, 2)
        xs, zs = (self.x + 2) % 4, (self.z + 2) % 4
        self.final = [f for j in range(2) for f in (xs * 4 + xs % 2 + 2 * j, ((zs + 1) % 2 + 2 * j) * 4 + zs)]

    def near(self, axis, d):
        along_z = self.x * 4 + (self.z + d) % 4
        along_x = (self.x + d) % 4 * 4 + self.z
        if isinstance(axis, int):
            return along_x if axis else along_z
        return jnp.where(axis == 0, along_z, along_x)

    def copy(self, k, f, part, phase, slot, to, src=None):
        s = 0 if self.once else k
        dst = self.at(k, f, part)
        return remote(dst if src is None else src, dst, self.sems[phase].at[s, slot], self.arrive.at[k, f], {"front": to})

    def arrival(self, k, f):
        return pltpu.make_async_copy(self.at(k, f, None), self.at(k, f, None), self.arrive.at[k, f])

    def plan(self, phase):
        x, z = self.x, self.z
        if phase == 0:
            return [(self.me, None, 0, self.near(self.parity, 1)), (self.me, None, 1, self.near(self.parity, 3))]
        if phase == 1:
            r = 1 - self.parity
            return [(self.near(r, 3), 0, 0, self.near(r, 1)), (self.near(r, 1), 1, 1, self.near(r, 3))]
        out = []
        if phase == 2:
            for j in range(2):
                f = x * 4 + x % 2 + 2 * j
                g = ((z + 1) % 2 + 2 * j) * 4 + z
                for d, i in ((1, 0), (3, 1)):
                    out.append((f, None, 4 * j + i, self.near(1, d)))
                for d, i in ((1, 2), (3, 3)):
                    out.append((g, None, 4 * j + i, self.near(0, d)))
            return out
        for j in range(2):
            for d, part in ((3, 0), (1, 1)):
                back = 4 - d
                xs, zs = (x + d) % 4, (z + d) % 4
                out.append((xs * 4 + xs % 2 + 2 * j, part, 4 * j + part, self.near(1, back)))
                out.append((((zs + 1) % 2 + 2 * j) * 4 + zs, part, 4 * j + 2 + part, self.near(0, back)))
        return out

    def start(self, phase, k, src=None):
        seen = None
        for f, part, slot, to in self.plans[phase]:
            new = f is not seen
            seen = f

            @self.when(k, f)
            def _():
                if new and phase in (1, 3):
                    self.arrival(k, f).wait()
                if new and phase == 2:
                    @pl.when(f == self.me)
                    def _():
                        self.own_ready(k)

                    @pl.when((f == self.opposite[0]) | (f == self.opposite[1]))
                    def _():
                        self.arrival(k, f).wait()
                if self.once:
                    @pl.when(k > 0)
                    def _():
                        self.copy(k - 1, f, part, phase, slot, to, src).wait_send()
                self.copy(k, f, part, phase, slot, to, src).start()

    def finish(self, k, lo, hi):
        for f in self.final:
            @pl.when(self.has(k, f) & (f >= lo) & (f < hi) if self.has else True)
            def _():
                self.arrival(k, f).wait()

    def when(self, k, f):
        if self.has:
            return pl.when(self.has(k, f))
        return lambda body: body()

    def prologue(self, first):
        first(0)
        self.start(1, 0)
        first(1)
        self.start(2, 0)
        self.start(1, 1)
        first(2)
        self.start(3, 0)
        self.start(2, 1)
        self.start(1, 2)
        first(3)

    def ahead(self, s, wide, first):
        j = s // 3

        @pl.when(s % 3 == 0)
        def _():
            @pl.when(j + 2 < wide)
            def _():
                self.start(2, j + 2)

            @pl.when(j + 3 < wide)
            def _():
                self.start(1, j + 3)

            @pl.when(j + 4 < wide)
            def _():
                first(j + 4)

        @pl.when((s % 3 == 1) & (j + 1 < wide))
        def _():
            self.start(3, j + 1)

    def drain(self, k, src=None):
        for phase in range(4):
            for f, part, slot, to in self.plans[phase]:
                @self.when(k, f)
                def _():
                    self.copy(k, f, part, phase, slot, to, src if phase == 0 else None).wait_send()


def square_sems(n):
    return [pltpu.SemaphoreType.DMA((n, c)) for c in (2, 2, 8, 8)]


def child_kernel(n, m, land, groups, a_ref, c_ref, hit_ref, l_out, c_out, reach, G, LG, own_sem, arrive, land_arrive, *more):
    sems, land_sems, scratch = more[:4], more[4:8], more[8:]
    T, Lh, Ll = scratch[0], scratch[1], scratch[2]
    stages, rows_own, wide = n // 128, n // groups, n // 256
    me = lax.axis_index("front")
    meet((("front", groups),))

    def part_of(ref, k, f, size, part):
        if part is None:
            return ref.at[k, dynamic(f, size), :]
        return ref.at[k, dynamic(2 * f + part, size // 2), :]

    def own_copy(k):
        return pltpu.make_async_copy(a_ref.at[:, dynamic(k, 256)], G.at[k, dynamic(me, rows_own), :], own_sem.at[k])

    def has(k, f):
        return f // 2 >= k
    rows = Square(lambda k, f, part: part_of(G, k, f, rows_own, part), arrive, sems, has, lambda k: own_copy(k).wait(), False)
    lands = Square(lambda k, f, part: part_of(LG, k, f, land, part), land_arrive, land_sems,
                   None, nothing, True)

    def first(k):
        rows.start(0, k, a_ref.at[:, dynamic(k, 256)])

        @pl.when(has(k, me))
        def _():
            own_copy(k).start()

    def land_use(k):
        lands.finish(k, 0, groups)
        cols = dynamic(k, 256)
        gh, gl = split(LG[k])
        reach[...] = reach[...] - dot3(Lh[n:n + m, cols], Ll[n:n + m, cols], gh, gl)

    def catch_up(p, late, long, short, body):
        def upto(q):
            return jnp.maximum(jnp.where(q >= late, (q - short) // 2, (q - long) // 2) + 1, 0)

        def step(q, _):
            body(q)
            return 0
        lax.fori_loop(upto(p - 1), upto(p), step, 0)

    rows.prologue(first)
    reach[...] = jnp.zeros_like(reach)

    def before(p):
        @pl.when(p % 2 == 0)
        def _():
            rows.finish(p // 2, p, p + 2)

    def after_factor(p):
        rows.ahead(2 * p, wide, first)
        catch_up(p, 12, 3, 2, lambda k: lands.start(1, k))
        catch_up(p, 13, 6, 3, lambda k: lands.start(3, k))

    def before_rest(p):
        @pl.when(p % 2 == 0)
        def _():
            rows.finish(p // 2, p + 2, groups)

    def stage(p, _):
        chol_stage(
            p, n, m,
            lambda kk, rows: G[kk, rows, :],
            lambda kk: c_ref[:, 256 * kk:256 * kk + 256],
            *scratch, before=before, after_factor=after_factor, before_rest=before_rest,
        )
        put_rows(p, n, m, rows_own, me * rows_own, T, l_out, c_out)
        k = p // 2

        @pl.when(p % 2 == 1)
        def _():
            cols = dynamic(k, 256)
            nn = functools.partial(jnp.dot, preferred_element_type=F32)
            LG[k, dynamic(me, land), :] = nn(hit_ref[...], Lh[n:n + m, cols]) + nn(hit_ref[...], Ll[n:n + m, cols])
        rows.ahead(2 * p + 1, wide, first)
        catch_up(p, 12, 4, 2, lambda k: lands.start(2, k))
        catch_up(p, 14, 7, 4, land_use)

        @pl.when(p % 2 == 1)
        def _():
            lands.start(0, k)
        return 0
    lax.fori_loop(0, stages, stage, 0)
    last = wide - 1
    lands.start(1, last)
    land_use(last - 1)
    lands.start(2, last)
    lands.start(3, last)
    land_use(last)
    lands.drain(last)

    def drain(k, _):
        rows.drain(k, a_ref.at[:, dynamic(k, 256)])
        return 0
    lax.fori_loop(0, wide, drain, 0)


def child_call(n, m, land, groups, side):
    dma = pltpu.SemaphoreType.DMA
    vmem = pl.BlockSpec(memory_space=pltpu.VMEM)
    return pl.pallas_call(
        functools.partial(child_kernel, n, m, land, groups),
        out_shape=[jax.ShapeDtypeStruct((n // groups, n), F32), jax.ShapeDtypeStruct((m, n), F32),
                   jax.ShapeDtypeStruct((m, land * groups), F32)],
        in_specs=[pl.BlockSpec(memory_space=pl.ANY), vmem, vmem],
        out_specs=[vmem] * 3,
        scratch_shapes=[
            pltpu.VMEM((n // 256, n, 256), F32), pltpu.VMEM((n // 256, land * groups, 256), F32),
            dma((n // 256,)), dma((n // 256, groups)), dma((n // 256, groups)),
        ] + square_sems(n // 256) + square_sems(1) + chol_scratch(n, m),
        compiler_params=pltpu.CompilerParams(vmem_limit_bytes=62 << 20, collective_id=0, has_side_effects=True),
    )


def parent_kernel(n, m, groups, bulks, reach, route, masked, out, PV, TP, RS, SB, RB, XH, XL, EH, EL,
                  scatter_send, scatter_come, gather_send, gather_come, spread_send, spread_come, arrive, *more):
    sems, scratch = more[:4], more[4:]
    T, Lh, Ll, U, E, ES, LS = scratch
    wide, full = n // 256, n // 128
    me, here = lax.axis_index("front"), lax.axis_index("bulk")
    meet((("front", groups), ("bulk", bulks)))
    nn = functools.partial(jnp.dot, preferred_element_type=F32)
    rh, rl = split(reach[...])

    def slot(b):
        r = route[b * m:(b + 1) * m, :]
        return nn(r, rh) + nn(r, rl)

    def other(d):
        return (here + d) % bulks

    def needed(j):
        return j // 2 <= me // 4

    def scatter(d):
        j = other(d)
        return remote(TP.at[j], RS.at[here], scatter_send.at[d - 1], scatter_come.at[here], {"bulk": j})

    def scattered(b):
        return pltpu.make_async_copy(RS.at[b], RS.at[b], scatter_come.at[b])

    def piece(j):
        return PV.at[j // 2, dynamic(me, m), dynamic(j % 2, 128)]

    def gather(d):
        return remote(piece(here), piece(here), gather_send.at[d - 1], gather_come.at[here], {"bulk": other(d)})

    def spread(d):
        b = other(d)
        return remote(SB.at[b], RB.at[here], spread_send.at[d - 1], spread_come.at[here], {"bulk": b})

    def spreaded(b):
        return pltpu.make_async_copy(RB.at[b], RB.at[b], spread_come.at[b])

    top = slot(0) + jnp.where(here == 0, masked[...], 0.0)
    for j in range(full):
        TP[j] = top[:, 128 * j:128 * j + 128]
    for d in range(1, bulks):
        @pl.when(needed(other(d)))
        def _():
            scatter(d).start()
    for b in range(1, bulks):
        SB[b] = slot(b)

    @pl.when(needed(here))
    def _():
        RS[here] = TP[here]
        for d in range(1, bulks):
            scattered(other(d)).wait()
        total = RS[0]
        for b in range(1, bulks):
            total = total + RS[b]
        PV[here // 2, dynamic(me, m), dynamic(here % 2, 128)] = total
        for d in range(1, bulks):
            gather(d).start()
    for d in range(1, bulks):
        j = other(d)

        @pl.when(needed(j))
        def _():
            pltpu.make_async_copy(piece(j), piece(j), gather_come.at[j]).wait()

    def part_at(k, f, part):
        if part is None:
            return PV.at[k, dynamic(f, m), :]
        return PV.at[k, dynamic(2 * f + part, m // 2), :]
    rows = Square(part_at, arrive, sems, lambda k, f: f // 4 >= k, nothing, False)

    def first(k):
        rows.start(0, k)
    first(0)
    first(1)
    rows.start(1, 0)
    rows.start(2, 0)
    for d in range(1, bulks):
        @pl.when(other(d) != 0)
        def _():
            spread(d).start()
    rows.start(1, 1)
    first(2)
    rows.start(3, 0)
    rows.start(2, 1)
    rows.start(1, 2)
    first(3)

    def before(p):
        @pl.when(p % 2 == 0)
        def _():
            rows.finish(p // 2, 2 * p, 2 * p + 4)

    def before_rest(p):
        @pl.when(p % 2 == 0)
        def _():
            rows.finish(p // 2, 2 * p + 4, groups)

    def stage(p, _):
        chol_stage(p, n, 0, lambda kk, r: PV[kk, r, :], None, *scratch, before=before,
                   after_factor=lambda p: rows.ahead(2 * p, wide, first), before_rest=before_rest)
        EH[p] = ES[0:128, 0:128]
        EL[p] = ES[128:256, 0:128]
        mine = T[dynamic(me, m), dynamic(p % 2, 128)]
        out[:, dynamic(p, 128)] = jnp.where(p * 128 < (me + 1) * m, mine, 0.0)
        rows.ahead(2 * p + 1, wide, first)
        return 0
    lax.fori_loop(0, full, stage, 0)

    @pl.when(here != 0)
    def _():
        for d in range(1, bulks):
            spreaded(other(d)).wait()
        RB[here] = SB[here]
        x = masked[...]
        for b in range(bulks):
            x = x + RB[b]
        for p in range(full):
            cols = slice(128 * p, 128 * p + 128)
            y = x[:, cols]
            if p:
                y = y - dot3(XH[:, :128 * p], XL[:, :128 * p], Lh[cols, :128 * p], Ll[cols, :128 * p])
            yh, yl = split(y)
            y = dot3(yh, yl, EH[p], EL[p])
            out[:, cols] = y
            yh, yl = split(y)
            XH[:, cols] = yh
            XL[:, cols] = yl
    for d in range(1, bulks):
        @pl.when(needed(other(d)))
        def _():
            scatter(d).wait_send()

        @pl.when(needed(here))
        def _():
            gather(d).wait_send()

        @pl.when(other(d) != 0)
        def _():
            spread(d).wait_send()

    def drain(k, _):
        rows.drain(k)
        return 0
    lax.fori_loop(0, wide, drain, 0)


def parent_call(n, m, groups, bulks):
    dma = pltpu.SemaphoreType.DMA
    vmem = pl.BlockSpec(memory_space=pltpu.VMEM)
    full, wide = n // 128, n // 256
    return pl.pallas_call(
        functools.partial(parent_kernel, n, m, groups, bulks),
        out_shape=jax.ShapeDtypeStruct((m, n), F32),
        in_specs=[vmem] * 3,
        out_specs=vmem,
        scratch_shapes=[
            pltpu.VMEM((wide, n, 256), F32), pltpu.VMEM((full, m, 128), F32), pltpu.VMEM((bulks, m, 128), F32),
            pltpu.VMEM((bulks, m, n), F32), pltpu.VMEM((bulks, m, n), F32), pltpu.VMEM((m, n), BF), pltpu.VMEM((m, n), BF),
            pltpu.VMEM((full, 128, 128), BF), pltpu.VMEM((full, 128, 128), BF),
            dma((bulks - 1,)), dma((bulks,)), dma((bulks - 1,)), dma((bulks,)), dma((bulks - 1,)), dma((bulks,)),
            dma((wide, groups)),
        ] + square_sems(wide) + chol_scratch(n, 0),
        compiler_params=pltpu.CompilerParams(vmem_limit_bytes=40 << 20, collective_id=1, has_side_effects=True),
    )


def on_device(child_pivot, child_coupling, parent_arrow, row_map, block_pattern):
    own_rows = child_pivot[0]
    parent_index = row_map[0]
    row_count, pivot_count = own_rows.shape
    parent_count, pivots = parent_arrow.shape
    front_index = lax.axis_index("front")
    front_groups = lax.axis_size("front")
    slot_index = (
        parent_index // parent_count // front_groups * parent_count + parent_index % parent_count
    )
    spread_rows = lax.axis_size("bulk") * parent_count
    routing = (jnp.arange(spread_rows)[:, None] == slot_index[None, :]).astype(BF)
    lower_rows, coupling, reached = child_call(pivot_count, row_count, parent_count, front_groups, 4)(
        own_rows, child_coupling[0], routing[:parent_count]
    )
    device_index = lax.axis_index("bulk") * front_groups + front_index
    first_row = device_index * parent_count
    block_rows = (first_row + jnp.arange(parent_count)) // BLOCK
    picker = (block_rows[:, None] == jnp.arange(block_pattern.shape[0])[None, :]).astype(F32)
    row_mask = jnp.dot(picker, block_pattern.astype(F32), precision=HIGHEST_PRECISION)
    masked = parent_arrow * jnp.repeat(row_mask, BLOCK, axis=1)
    parent_rows = parent_call(pivots, parent_count, front_groups, lax.axis_size("bulk"))(reached, routing, masked)
    return (lower_rows[None], coupling[None], parent_rows)


def solution(mesh):
    placed = (
        P("bulk", "front", None),
        P("bulk", "front", None),
        P(("bulk", "front"), None),
        P("bulk", "front"),
        P(),
    )
    return jax.shard_map(
        on_device,
        mesh=mesh,
        in_specs=placed,
        out_specs=(P("bulk", "front", None), P("bulk", "front", None), P(("bulk", "front"), None)),
        check_vma=False,
    )
```
